512 devices in a mesh: space: 32 (over y, z_lo), chan: 16 (over x, z_hi, core).
Axes of the slice: x: 4, y: 4, z: 16 (z_hi: 2, z_lo: 8; z = z_hi * 8 + z_lo), core: 2. Of those that a mesh axis runs over, the one named last changes fastest.
Arguments:
- latent: bfloat16 [1, 32, 160, 512], P(None, 'space', None, 'chan'), may hold values from -12 to 12
- cache_mid: bfloat16 [2, 32, 160, 512], P(None, 'space', None, 'chan'), may hold values from -6 to 6
- norm1_gain: float32 [512], P('chan'), may hold values from 0.1 to 1.9
- norm1_bias: float32 [512], P('chan'), may hold values from -3 to 3
- conv1_weight: bfloat16 [3, 3, 3, 512, 512], P(None, None, None, 'chan'), may hold values from -0.0625 to 0.0625
- conv1_bias: float32 [512], P('chan'), may hold values from -2 to 2
- cache_up: bfloat16 [2, 64, 320, 512], P(None, 'space', 'chan'), may hold values from -6 to 6
- norm2_gain: float32 [512], replicated, may hold values from 0.1 to 1.9
- norm2_bias: float32 [512], replicated, may hold values from -3 to 3
- conv2_weight: bfloat16 [3, 3, 3, 512, 512], P(None, None, None, None, 'chan'), may hold values from -0.0546875 to 0.0546875
- conv2_bias: float32 [512], replicated, may hold values from -2 to 2
Outputs:
- up_features: bfloat16 [1, 64, 320, 512], P(None, 'space', 'chan')
The draws below stay inside these ranges and needn't reach their ends.
All inputs are finite; a program needn't handle non-finite values.
Results may differ from the reference program's by a relative error of at most 0.0038.
The reference program's roundings to bfloat16 on the way (of `normed_mid`, `merged`, `upsampled` and `normed_up`) count: a program that leaves them out, or rounds other values in their place, can miss the bound.
Values may be sent and summed in bfloat16 or wider, within the bound.
No kernel may reach another device: no remote copies, remote signals or barrier semaphores. Data moves between devices by JAX's collectives and lax.ppermute only.
A program may use at most 64 MiB of HBM per device.

```python
import jax
import jax.numpy as jnp
from jax import lax

CH = 512
GROUPS = 32
FRAMES = 1
W = 160
GS = 16
H = 32
H2 = 64
W2 = 320


def draw_latent(key, part):
    first_key, second_key, rough_key, offset_key = jax.random.split(key, 4)
    row_place = jnp.arange(H, dtype=jnp.float32) / max(H - 1, 1)
    row_rough = jnp.exp(jax.random.uniform(rough_key, (H,), jnp.float32, -1.0, 1.0))
    base = jax.random.normal(first_key, (FRAMES, H, W, CH), jnp.float32)
    row_scale = 0.4 * 3.0 ** row_place * row_rough
    row_offset = jax.random.uniform(offset_key, (H,), jnp.float32, -1.5, 1.5)
    chan_scale = jnp.exp(jax.random.uniform(second_key, (CH,), jnp.float32, -0.7, 0.7))
    drawn = base * row_scale[None, :, None, None] * chan_scale + row_offset[None, :, None, None]
    return jnp.clip(drawn, -12.0, 12.0).astype(jnp.bfloat16)


def with_spikes(entries, key, source, target, parts, factor):
    owner, partner = [(jnp.arange(entries.shape[axis_at]) // (entries.shape[axis_at] // parts)).reshape([-1 if axis == axis_at else 1 for axis in range(entries.ndim)]) for axis_at in (source, target)]
    chosen = jax.random.permutation(key, parts)[partner]
    strong = (owner == chosen) | (owner == (partner + parts // 2) % parts)
    return jnp.where(strong, factor * entries, entries)


def block_scale(key, dims, cuts, smallest, high):
    def one(position, blocks):
        steps = jax.random.uniform(jax.random.fold_in(jax.random.fold_in(key, 6), position), (blocks,), jnp.float32, smallest / len(cuts), high / len(cuts))
        return jnp.repeat(jnp.exp(steps), dims[position] // blocks).reshape((-1,) + (1,) * (len(dims) - position - 1))

    loudness = one(*cuts[0])
    for cut in cuts[1:]:
        loudness = loudness * one(*cut)
    return loudness


def normal_values(own_key, shape, spread, reach, shards=(), held_as=jnp.bfloat16):
    values = spread * jax.random.normal(own_key, shape, jnp.float32)
    if shards:
        values = values * block_scale(own_key, shape, shards, -0.22, 0.18)
    return jnp.clip(values, -reach, reach).astype(held_as)


def noise_with(own_key, dims, width, bound, pieces, heavy, kind=jnp.bfloat16):
    values = width * jax.random.normal(own_key, dims, jnp.float32)
    if pieces:
        values = values * block_scale(own_key, dims, pieces, -0.22, 0.18)
    return jnp.clip(with_spikes(values, jax.random.fold_in(own_key, 3), *heavy), -bound, bound).astype(kind)


def setup_inputs(seed: int = 0) -> dict:
    keys = jax.random.split(jax.random.key(seed), 12)
    latent = draw_latent(jax.random.fold_in(keys[11], 71), 0)
    cache_mid = normal_values(keys[1], (2, H, W, CH), 1.0, 6.0, ((1, 32), (3, 16)))
    norm1_gain = jnp.clip(1.0 + 0.18 * jax.random.normal(keys[2], (CH,), jnp.float32), 0.1, 1.9)
    norm1_bias = normal_values(keys[3], (CH,), 0.5, 3.0, ((0, 16),), jnp.float32)
    conv1_weight = noise_with(keys[4], (3, 3, 3, CH, CH), (27 * CH) ** -0.5, 0.0625, ((3, 16),), (3, 4, 16, 2.0))
    conv1_bias = normal_values(keys[5], (CH,), 0.3, 2.0, ((0, 16),), jnp.float32)
    cache_up = normal_values(keys[6], (2, H2, W2, CH), 1.0, 6.0, ((1, 32), (2, 16)))
    norm2_gain = jnp.clip(1.0 + 0.18 * jax.random.normal(keys[7], (CH,), jnp.float32), 0.1, 1.9)
    norm2_bias = normal_values(keys[8], (CH,), 0.5, 3.0, (), jnp.float32)
    conv2_weight = normal_values(keys[9], (3, 3, 3, CH, CH), (27 * CH) ** -0.5, 0.0546875, ((4, 16),))
    conv2_bias = normal_values(keys[10], (CH,), 0.3, 2.0, (), jnp.float32)
    return dict(latent=latent, cache_mid=cache_mid, norm1_gain=norm1_gain, norm1_bias=norm1_bias, conv1_weight=conv1_weight, conv1_bias=conv1_bias, cache_up=cache_up, norm2_gain=norm2_gain, norm2_bias=norm2_bias, conv2_weight=conv2_weight, conv2_bias=conv2_bias)


epsilon = 1e-06

def norm_silu(values, gain, bias):
    layout_shape = values.shape
    grouped = values.reshape(layout_shape[:-1] + (GROUPS, GS))
    group_mean = lax.optimization_barrier(jnp.mean(grouped, axis=(0, 1, 2, 4), keepdims=True))
    centred = grouped - group_mean
    group_var = lax.optimization_barrier(jnp.mean(centred * centred, axis=(0, 1, 2, 4), keepdims=True))
    scaled = (centred * lax.rsqrt(group_var + epsilon)).reshape(layout_shape)
    return jax.nn.silu(scaled * gain + bias)

def causal_conv(sequence, kernel):
    result = lax.conv_general_dilated(sequence.astype(jnp.float32)[None], kernel.astype(jnp.float32), (1, 1, 1), ((0, 0), (1, 1), (1, 1)), dimension_numbers=('NDHWC', 'DHWIO', 'NDHWC'), precision=lax.Precision.HIGHEST)
    return result[0]

def reference(latent, cache_mid, norm1_gain, norm1_bias, conv1_weight, conv1_bias, cache_up, norm2_gain, norm2_bias, conv2_weight, conv2_bias):
    values = latent.astype(jnp.float32)
    normed_mid = norm_silu(values, norm1_gain, norm1_bias).astype(jnp.bfloat16)
    conv_mid = causal_conv(jnp.concatenate([cache_mid, normed_mid], axis=0), conv1_weight)
    merged = (values + conv_mid + conv1_bias).astype(jnp.bfloat16)
    upsampled = jnp.repeat(jnp.repeat(merged, 2, axis=1), 2, axis=2)
    normed_up = norm_silu(upsampled.astype(jnp.float32), norm2_gain, norm2_bias).astype(jnp.bfloat16)
    up_conv = causal_conv(jnp.concatenate([cache_up, normed_up], axis=0), conv2_weight)
    return (up_conv + conv2_bias).astype(jnp.bfloat16)
```

```python
import functools

import jax
import jax.numpy as jnp
from jax import lax
from jax.experimental import pallas as pl
from jax.experimental.pallas import tpu as pltpu
from jax.sharding import Mesh
from jax.sharding import PartitionSpec as P

GS = 16
EPS = 1e-06
F32 = jnp.float32
BF16 = jnp.bfloat16
USE_KERNELS = True


def run(fn, out_shapes, args, scalars=(), name=None):
    if not USE_KERNELS:
        return fn(*scalars, *args)
    n_s, n_a, single = len(scalars), len(args), isinstance(out_shapes, tuple)
    shapes = [out_shapes] if single else list(out_shapes)

    def body(*refs):
        ins = list(refs[:n_s]) + [r[...] for r in refs[n_s : n_s + n_a]]
        outs = fn(*ins)
        outs = [outs] if single else outs
        for ref, value in zip(refs[n_s + n_a :], outs):
            ref[...] = value

    vmem = pl.BlockSpec(memory_space=pltpu.VMEM)
    res = pl.pallas_call(
        body,
        out_shape=[jax.ShapeDtypeStruct(s, d) for s, d in shapes],
        in_specs=[pl.BlockSpec(memory_space=pltpu.SMEM)] * n_s + [vmem] * n_a,
        out_specs=[vmem] * len(shapes),
        name=name,
    )(*scalars, *args)
    return res[0] if single else res


def to_row(col):
    n = col.shape[0]
    eye = lax.broadcasted_iota(jnp.int32, (n, n), 0) == lax.broadcasted_iota(jnp.int32, (n, n), 1)
    return jnp.sum(jnp.where(eye, col, 0.0), axis=0, keepdims=True)


def to_col(row, repeat):
    n = row.shape[1]
    rows = lax.broadcasted_iota(jnp.int32, (n * repeat, n), 0)
    lanes = lax.broadcasted_iota(jnp.int32, (n * repeat, n), 1)
    pick = (rows >= lanes * repeat) & (rows < lanes * repeat + repeat)
    return jnp.sum(jnp.where(pick, row, 0.0), axis=1, keepdims=True)


def partial_stats(values, peers):
    rows, cols = values.shape
    groups = rows // GS
    x = values.astype(F32)
    mean = jnp.sum(jnp.sum(x, axis=1, keepdims=True).reshape(groups, GS, 1), axis=1) / (GS * cols)
    dev = x.reshape(groups, GS, cols) - mean[:, :, None]
    sq = jnp.sum(jnp.sum(dev * dev, axis=2, keepdims=True), axis=1)
    row = jnp.concatenate(
        [to_row(mean), to_row(sq), jnp.zeros((1, 128 - 2 * groups), F32)], axis=1
    )
    return jnp.broadcast_to(row[None], (peers, 1, 128))


def merge_stats(parts, groups, count):
    peers = parts.shape[0]
    means = parts[:, 0, :groups]
    sq = parts[:, 0, groups : 2 * groups]
    mean = jnp.sum(means, axis=0, keepdims=True) / peers
    gap = means - mean
    var = (jnp.sum(sq, axis=0, keepdims=True) + count * jnp.sum(gap * gap, axis=0, keepdims=True)) / (
        count * peers
    )
    return mean, lax.rsqrt(var + EPS)


def norm_silu(x, mean, scale, gain, bias):
    v = (x.astype(F32) - mean) * scale * gain + bias
    low = v < -80.0
    e = jnp.exp(jnp.where(low, v, -v))
    return jnp.where(low, v * e, v / (1.0 + jnp.where(low, 0.0, e)))


def right(a):
    return jnp.concatenate([jnp.zeros((a.shape[0], 1), a.dtype), a[:, :-1]], axis=1)


def left(a):
    return jnp.concatenate([a[:, 1:], jnp.zeros((a.shape[0], 1), a.dtype)], axis=1)


def mid_conv(place, parts, raw, above, below, gain, bias, kernel):
    chans, cols = raw.shape[1:]
    groups = chans // GS
    mean, scale = merge_stats(parts, groups, GS * cols)
    mean, scale = to_col(mean, GS), to_col(scale, GS)
    pieces = []
    for t in range(3):
        for dy, src in enumerate((above, raw, below)):
            x = src[t].astype(F32)
            if t == 2:
                x = norm_silu(x, mean, scale, gain, bias)
                if dy != 1:
                    x = jnp.where(place[0 if dy == 0 else 1] == 1, x, 0.0)
            pieces += [right(x).astype(BF16), x.astype(BF16), left(x).astype(BF16)]
    columns = jnp.concatenate(pieces, axis=0)
    out = jnp.dot(kernel, columns, preferred_element_type=F32)
    return out.reshape(8, out.shape[0] // 8, cols)


def fold(place, parts, own, bias):
    total = jnp.sum(parts, axis=0)
    half = total.shape[0] // 2
    extra = own.astype(F32) + bias
    zero = jnp.zeros_like(extra)
    first = place[2] == 0
    return total + jnp.concatenate(
        [jnp.where(first, extra, zero), jnp.where(first, zero, extra)], axis=0
    )


def row_stats(gathered, peers):
    cols = gathered.shape[2]
    blocks = gathered.reshape(4, 2, 2, 32, cols)
    row = jnp.concatenate(
        [blocks[x, k, h] for x in range(4) for h in range(2) for k in range(2)], axis=0
    )
    return row, partial_stats(row, peers)


def taps(prod):
    return [[prod[(dy * 3 + dx) * 32 : (dy * 3 + dx + 1) * 32] for dx in range(3)] for dy in range(3)]


def cache_conv(images, kernel):
    per = 9 * 32
    sums = {}

    def add(key, value):
        sums[key] = sums[key] + value if key in sums else value

    for t in range(2):
        w = kernel[t * per : (t + 1) * per]
        for r in range(2):
            even, odd = (
                taps(
                    lax.dot_general(
                        w, images[t, r, p], (((1,), (1,)), ((), ())), preferred_element_type=F32
                    )
                )
                for p in range(2)
            )
            for dy in range(3):
                o = r + 1 - dy
                add((o, "m", 0), even[dy][1] + odd[dy][2])
                add((o, "r", 0), odd[dy][0])
                add((o, "m", 1), even[dy][0] + odd[dy][1])
                add((o, "l", 1), even[dy][2])

    def out(o):
        return jnp.concatenate(
            [
                sums[(o, "m", 0)] + right(sums[(o, "r", 0)]),
                sums[(o, "m", 1)] + left(sums[(o, "l", 1)]),
            ],
            axis=0,
        )

    return jnp.concatenate([out(0), out(1)], axis=0), out(-1), out(2)


def up_conv(place, parts, row, above, below, gain, bias, kernel, held, from_above, from_below, out_bias):
    chans, cols = row.shape
    groups = chans // GS
    mean, scale = merge_stats(parts, groups, GS * cols)
    mean, scale = to_col(mean, GS), to_col(scale, GS)
    per = 9 * 32
    w = kernel[2 * per :]

    def image(x, keep=None):
        v = norm_silu(x, mean, scale, gain, bias)
        if keep is not None:
            v = jnp.where(keep == 1, v, 0.0)
        return v.astype(BF16)

    lhs = jnp.concatenate([w[dy * 3 * 32 : (dy + 1) * 3 * 32] for dy in range(3)], axis=1)
    here = image(row)
    outs = []
    for images in (
        (image(above, place[0]), here, here),
        (here, here, image(below, place[1])),
    ):
        prod = jnp.dot(lhs, jnp.concatenate(images, axis=0), preferred_element_type=F32)
        cut = [prod[dx * 32 : (dx + 1) * 32] for dx in range(3)]
        outs += [right(cut[0]) + cut[1] + cut[2], cut[0] + cut[1] + left(cut[2])]
    total = jnp.concatenate(outs, axis=0) + held
    total = total + jnp.concatenate([from_above, from_below], axis=0) + out_bias
    return total.T.astype(BF16)


def on_device(
    sizes,
    latent,
    cache_mid,
    norm1_gain,
    norm1_bias,
    conv1_weight,
    conv1_bias,
    cache_up,
    norm2_gain,
    norm2_bias,
    conv2_weight,
    conv2_bias,
):
    n_y, n_l = sizes
    peers = n_y * n_l
    cols, chans = latent.shape[2], latent.shape[3]
    place_s = lax.axis_index(("y", "l"))
    hi = lax.axis_index("h")
    chan = lax.axis_index(("x", "h", "k"))
    place = jnp.stack(
        [(place_s > 0).astype(jnp.int32), (place_s < peers - 1).astype(jnp.int32), hi.astype(jnp.int32)]
    )
    space = ("y", "l")
    own = latent[0, 0].T
    stats = run(
        functools.partial(partial_stats, peers=peers), ((peers, 1, 128), F32), (own,), name="stats_mid"
    )
    stats = lax.all_to_all(stats, space, 0, 0, tiled=True)
    raw = jnp.concatenate([cache_mid[:, 0], latent[0]], axis=0).transpose(0, 2, 1)
    down = [(i, i + 1) for i in range(peers - 1)]
    up = [(i + 1, i) for i in range(peers - 1)]
    above = lax.ppermute(raw, space, down)
    below = lax.ppermute(raw, space, up)
    kernel1 = conv1_weight.reshape(27 * chans, 4, 2, 2, 32).transpose(1, 3, 2, 4, 0).reshape(512, -1)
    partial = run(
        mid_conv,
        ((8, 64, cols), F32),
        (stats, raw, above, below, norm1_gain[:, None], norm1_bias[:, None], kernel1),
        (place,),
        name="mid_conv",
    )
    partial = lax.all_to_all(partial, ("x", "k"), 0, 0, tiled=True)
    mine = run(fold, ((64, cols), F32), (partial, own, conv1_bias[:, None]), (place,), name="fold")
    other = lax.ppermute(mine, "h", [(0, 1), (1, 0)])
    merged = (mine + other).astype(BF16)
    gathered = lax.all_to_all(
        jnp.broadcast_to(merged[None], (8, 64, cols)), ("x", "k"), 0, 0, tiled=True
    )
    row, stats2 = run(
        functools.partial(row_stats, peers=peers),
        [((512, cols), BF16), ((peers, 1, 128), F32)],
        (gathered,),
        name="row_stats",
    )
    stats2 = lax.all_to_all(stats2, space, 0, 0, tiled=True)

    def at(y, l, h):
        return (y * n_l + l) * 2 + h

    down_h, up_h = [], []
    for y in range(n_y):
        for l in range(n_l):
            for h in range(2):
                if l < n_l - 1:
                    pair = (at(y, l, h), at(y, l + 1, h))
                elif y < n_y - 1:
                    pair = (at(y, l, h), at(y + 1, 0, 1 - h))
                else:
                    continue
                down_h.append(pair)
                up_h.append(pair[::-1])
    row_above = lax.ppermute(row, ("y", "l", "h"), down_h)
    row_below = lax.ppermute(row, ("y", "l", "h"), up_h)

    tile = cache_up.reshape(2, 2, 10, 2, 512).transpose(0, 1, 3, 2, 4)
    swapped = lax.ppermute(tile, "h", [(0, 1), (1, 0)])
    pair = jnp.where(hi == 0, jnp.stack([tile, swapped]), jnp.stack([swapped, tile]))
    spread = lax.all_to_all(
        jnp.broadcast_to(pair[None], (8,) + pair.shape), ("x", "k"), 0, 0, tiled=True
    )
    images = (
        spread.reshape(4, 2, 2, 2, 2, 2, 10, 512)
        .transpose(3, 4, 5, 0, 2, 1, 6, 7)
        .reshape(2, 2, 2, cols, 512)
    )
    kernel2 = conv2_weight.transpose(0, 1, 2, 4, 3).reshape(27 * 32, 512)
    held, to_above, to_below = run(
        cache_conv,
        [((128, cols), F32), ((64, cols), F32), ((64, cols), F32)],
        (images, kernel2),
        name="cache_conv",
    )
    from_above = lax.ppermute(to_below, space, down)
    from_below = lax.ppermute(to_above, space, up)
    bias_here = lax.dynamic_slice_in_dim(conv2_bias, chan * 32, 32)
    out = run(
        up_conv,
        ((cols, 128), BF16),
        (
            stats2,
            row,
            row_above,
            row_below,
            norm2_gain[:, None],
            norm2_bias[:, None],
            kernel2,
            held,
            from_above,
            from_below,
            jnp.tile(bias_here, 4)[:, None],
        ),
        (place,),
        name="up_conv",
    )
    out = lax.all_to_all(out.reshape(16, 10, 128), ("x", "h", "k"), 0, 0, tiled=True)
    out = out.reshape(16, 10, 2, 2, 32).transpose(2, 1, 3, 0, 4)
    return out.reshape(1, 2, 20, 512)


def solution(mesh):
    peers = mesh.shape["space"]
    n_l = 8 if peers % 8 == 0 else 2
    n_y = peers // n_l
    fine = Mesh(mesh.devices.reshape(n_y, n_l, 4, 2, 2), ("y", "l", "x", "h", "k"))
    space, chan = ("y", "l"), ("x", "h", "k")
    placed = (
        P(None, space, None, chan),
        P(None, space, None, chan),
        P(chan),
        P(chan),
        P(None, None, None, chan, None),
        P(chan),
        P(None, space, chan, None),
        P(),
        P(),
        P(None, None, None, None, chan),
        P(),
    )
    return jax.shard_map(
        functools.partial(on_device, (n_y, n_l)),
        mesh=fine,
        in_specs=placed,
        out_specs=P(None, space, chan, None),
        check_vma=False,
    )
```

```python
import functools

import jax
import jax.numpy as jnp
from jax import lax
from jax.experimental import pallas as pl
from jax.experimental.pallas import tpu as pltpu
from jax.sharding import Mesh
from jax.sharding import PartitionSpec as P

GS = 16
EPS = 1e-06
F32 = jnp.float32
BF16 = jnp.bfloat16
USE_KERNELS = True


def run(fn, out_shapes, args, name, grant=8):
    if not USE_KERNELS:
        return fn(*args)
    n_a, single = len(args), isinstance(out_shapes, tuple)
    shapes = [out_shapes] if single else list(out_shapes)

    def body(*refs):
        outs = fn(*[r[...] for r in refs[:n_a]])
        outs = [outs] if single else outs
        for ref, value in zip(refs[n_a:], outs):
            ref[...] = value

    vmem = pl.BlockSpec(memory_space=pltpu.VMEM)
    res = pl.pallas_call(
        body,
        out_shape=[jax.ShapeDtypeStruct(s, d) for s, d in shapes],
        in_specs=[vmem] * n_a,
        out_specs=[vmem] * len(shapes),
        name=name,
        compiler_params=pltpu.CompilerParams(vmem_limit_bytes=grant << 20),
    )(*args)
    return res[0] if single else res


def to_row(col):
    n = col.shape[0]
    eye = lax.broadcasted_iota(jnp.int32, (n, n), 0) == lax.broadcasted_iota(jnp.int32, (n, n), 1)
    return jnp.sum(jnp.where(eye, col, 0.0), axis=0, keepdims=True)


def to_col(row, repeat):
    n = row.shape[1]
    rows = lax.broadcasted_iota(jnp.int32, (n * repeat, n), 0)
    lanes = lax.broadcasted_iota(jnp.int32, (n * repeat, n), 1)
    pick = (rows >= lanes * repeat) & (rows < lanes * repeat + repeat)
    return jnp.sum(jnp.where(pick, row, 0.0), axis=1, keepdims=True)


def partial_stats(values, peers):
    rows, cols = values.shape
    groups = rows // GS
    x = values.astype(F32)
    mean = jnp.sum(jnp.sum(x, axis=1, keepdims=True).reshape(groups, GS, 1), axis=1) / (GS * cols)
    dev = x.reshape(groups, GS, cols) - mean[:, :, None]
    sq = jnp.sum(jnp.sum(dev * dev, axis=2, keepdims=True), axis=1)
    row = jnp.concatenate(
        [to_row(mean), to_row(sq), jnp.zeros((1, 128 - 2 * groups), F32)], axis=1
    )
    return jnp.broadcast_to(row[None], (peers, 1, 128))


def merge_stats(parts, groups, count):
    peers = parts.shape[0]
    means = parts[:, 0, :groups]
    sq = parts[:, 0, groups : 2 * groups]
    mean = jnp.sum(means, axis=0, keepdims=True) / peers
    gap = means - mean
    var = (jnp.sum(sq, axis=0, keepdims=True) + count * jnp.sum(gap * gap, axis=0, keepdims=True)) / (
        count * peers
    )
    return mean, lax.rsqrt(var + EPS)


def norm_silu(x, mean, scale, gain, bias):
    v = (x.astype(F32) - mean) * scale * gain + bias
    low = v < -80.0
    e = jnp.exp(jnp.where(low, v, -v))
    return jnp.where(low, v * e, v / (1.0 + jnp.where(low, 0.0, e)))


def wide_col(row):
    n = row.shape[1]
    return jnp.concatenate([to_col(row[:, i : i + 128], 1) for i in range(0, n, 128)], axis=0)


def pack(a):
    tail = jnp.concatenate([a[16 * i : 16 * i + 16, 128:] for i in range(4)], axis=1)
    return jnp.concatenate([a[:, :128], tail], axis=0)


def unpack(a):
    tail = jnp.concatenate([a[64:, 32 * i : 32 * i + 32] for i in range(4)], axis=0)
    return jnp.concatenate([a[:64], tail], axis=1)


def right(a):
    return jnp.concatenate([jnp.zeros((a.shape[0], 1), a.dtype), a[:, :-1]], axis=1)


def left(a):
    return jnp.concatenate([a[:, 1:], jnp.zeros((a.shape[0], 1), a.dtype)], axis=1)


def edges(sizes):
    n_y, n_l = sizes
    row = lax.axis_index("y") * n_l + lax.axis_index("l")
    return row > 0, row < n_y * n_l - 1


def first_pass(own, cache, peers):
    return partial_stats(own, peers), jnp.concatenate([cache, own[None]], axis=0)


def mid_conv(parts, raw, above, below, gain, bias, kernel, sizes):
    chans, cols = raw.shape[1:]
    groups = chans // GS
    mean, scale = merge_stats(parts, groups, GS * cols)
    mean, scale = to_col(mean, GS), to_col(scale, GS)
    gain, bias = to_col(gain, 1), to_col(bias, 1)
    has = edges(sizes)
    pieces = []
    for t in range(3):
        for dy, src in enumerate((above, raw, below)):
            x = src[t].astype(F32)
            if t == 2:
                x = norm_silu(x, mean, scale, gain, bias)
                if dy != 1:
                    x = jnp.where(has[0 if dy == 0 else 1], x, 0.0)
            pieces += [right(x).astype(BF16), x.astype(BF16), left(x).astype(BF16)]
    columns = jnp.concatenate(pieces, axis=0)
    out = jnp.dot(columns.T, kernel, preferred_element_type=F32).T
    blocks = []
    for x in range(4):
        for k in range(2):
            both = [out[(x * 4 + h * 2 + k) * 32 :][:32] for h in range(2)]
            blocks.append(pack(jnp.concatenate(both, axis=0)))
    return jnp.stack(blocks)


def fold(parts, own, bias):
    total = unpack(jnp.sum(parts, axis=0))
    extra = own.astype(F32) + to_col(bias, 1)
    zero = jnp.zeros_like(extra)
    first = lax.axis_index("h") == 0
    return pack(
        total
        + jnp.concatenate([jnp.where(first, extra, zero), jnp.where(first, zero, extra)], axis=0)
    )


def merge(mine, other):
    merged = (mine + other).astype(BF16)
    return jnp.broadcast_to(merged[None], (8,) + merged.shape)


def rows_of(gathered):
    blocks = [unpack(gathered[i].astype(F32)) for i in range(8)]
    return jnp.concatenate(
        [
            blocks[x * 2 + k][h * 32 : (h + 1) * 32]
            for x in range(4)
            for h in range(2)
            for k in range(2)
        ],
        axis=0,
    )


def row_stats(gathered, peers):
    return partial_stats(rows_of(gathered), peers)


def taps(prod):
    return [[prod[(dy * 3 + dx) * 32 : (dy * 3 + dx + 1) * 32] for dx in range(3)] for dy in range(3)]


def cache_conv(images, kernel):
    per = 9 * 32
    sums = {}

    def add(key, value):
        sums[key] = sums[key] + value if key in sums else value

    for t in range(2):
        w = kernel[t * per : (t + 1) * per]
        for r in range(2):
            even, odd = (
                taps(
                    lax.dot_general(
                        w, images[t, r, p], (((1,), (1,)), ((), ())), preferred_element_type=F32
                    )
                )
                for p in range(2)
            )
            for dy in range(3):
                o = r + 1 - dy
                add((o, "m", 0), even[dy][1] + odd[dy][2])
                add((o, "r", 0), odd[dy][0])
                add((o, "m", 1), even[dy][0] + odd[dy][1])
                add((o, "l", 1), even[dy][2])

    def out(o):
        return jnp.concatenate(
            [
                sums[(o, "m", 0)] + right(sums[(o, "r", 0)]),
                sums[(o, "m", 1)] + left(sums[(o, "l", 1)]),
            ],
            axis=0,
        )

    return jnp.concatenate([out(0), out(1)], axis=0), out(-1), out(2)


def up_conv(parts, row, above, below, gain, bias, kernel, held, from_above, from_below, out_bias, sizes):
    row, above, below = rows_of(row), rows_of(above), rows_of(below)
    chans, cols = row.shape
    groups = chans // GS
    mean, scale = merge_stats(parts, groups, GS * cols)
    mean, scale = to_col(mean, GS), to_col(scale, GS)
    gain, bias = wide_col(gain), wide_col(bias)
    has = edges(sizes)
    per = 9 * 32
    w = kernel[2 * per :]

    def image(x, keep=None):
        v = norm_silu(x, mean, scale, gain, bias)
        if keep is not None:
            v = jnp.where(keep, v, 0.0)
        return v.astype(BF16)

    lhs = jnp.concatenate([w[dy * 3 * 32 : (dy + 1) * 3 * 32] for dy in range(3)], axis=1)
    here = image(row)
    outs = []
    for images in ((image(above, has[0]), here, here), (here, here, image(below, has[1]))):
        prod = jnp.dot(lhs, jnp.concatenate(images, axis=0), preferred_element_type=F32)
        cut = [prod[dx * 32 : (dx + 1) * 32] for dx in range(3)]
        outs += [right(cut[0]) + cut[1] + cut[2], cut[0] + cut[1] + left(cut[2])]
    total = jnp.concatenate(outs, axis=0) + held
    chan = lax.axis_index("x") * 4 + lax.axis_index("h") * 2 + lax.axis_index("k")
    rows = lax.broadcasted_iota(jnp.int32, (32, chans), 0)
    lanes = lax.broadcasted_iota(jnp.int32, (32, chans), 1)
    picked = jnp.sum(jnp.where(lanes == rows + chan * 32, out_bias, 0.0), axis=1, keepdims=True)
    total = total + jnp.concatenate([from_above, from_below], axis=0)
    total = (total + jnp.concatenate([picked] * 4, axis=0)).T
    part = cols // 16
    return jnp.stack([total[c * part : (c + 1) * part] for c in range(16)]).astype(BF16)


def on_device(
    sizes,
    latent,
    cache_mid,
    norm1_gain,
    norm1_bias,
    conv1_weight,
    conv1_bias,
    cache_up,
    norm2_gain,
    norm2_bias,
    conv2_weight,
    conv2_bias,
):
    n_y, n_l = sizes
    peers = n_y * n_l
    cols, chans = latent.shape[2], latent.shape[3]
    sizes = (n_y, n_l)
    hi = lax.axis_index("h")
    space = ("y", "l")
    own = latent[0, 0].T
    stats, raw = run(
        functools.partial(first_pass, peers=peers),
        [((peers, 1, 128), F32), ((3, chans, cols), BF16)],
        (own, cache_mid[:, 0].transpose(0, 2, 1)),
        "first_pass",
    )
    stats = lax.all_to_all(stats, space, 0, 0, tiled=True)
    down = [(i, i + 1) for i in range(peers - 1)]
    up = [(i + 1, i) for i in range(peers - 1)]
    above = lax.ppermute(raw, space, down)
    below = lax.ppermute(raw, space, up)
    partial = run(
        functools.partial(mid_conv, sizes=sizes),
        ((8, 80, 128), F32),
        (stats, raw, above, below, norm1_gain[None], norm1_bias[None], conv1_weight.reshape(27 * chans, 512)),
        "mid_conv",
    )
    partial = lax.all_to_all(partial, ("x", "k"), 0, 0, tiled=True)
    mine = run(fold, ((80, 128), F32), (partial, own, conv1_bias[None]), "fold")
    other = lax.ppermute(mine, "h", [(0, 1), (1, 0)])
    gathered = run(merge, ((8, 80, 128), BF16), (mine, other), "merge")
    gathered = lax.all_to_all(gathered, ("x", "k"), 0, 0, tiled=True)
    stats2 = run(
        functools.partial(row_stats, peers=peers), ((peers, 1, 128), F32), (gathered,), "row_stats"
    )
    stats2 = lax.all_to_all(stats2, space, 0, 0, tiled=True)

    def at(y, l, h):
        return (y * n_l + l) * 2 + h

    down_h, up_h = [], []
    for y in range(n_y):
        for l in range(n_l):
            for h in range(2):
                if l < n_l - 1:
                    pair = (at(y, l, h), at(y, l + 1, h))
                elif y < n_y - 1:
                    pair = (at(y, l, h), at(y + 1, 0, 1 - h))
                else:
                    continue
                down_h.append(pair)
                up_h.append(pair[::-1])
    row_above = lax.ppermute(gathered, ("y", "l", "h"), down_h)
    row_below = lax.ppermute(gathered, ("y", "l", "h"), up_h)

    tile = cache_up.reshape(2, 2, 10, 2, 512).transpose(0, 1, 3, 2, 4)
    swapped = lax.ppermute(tile, "h", [(0, 1), (1, 0)])
    pair = jnp.where(hi == 0, jnp.stack([tile, swapped]), jnp.stack([swapped, tile]))
    spread = lax.all_to_all(
        jnp.broadcast_to(pair[None], (8,) + pair.shape), ("x", "k"), 0, 0, tiled=True
    )
    images = (
        spread.reshape(4, 2, 2, 2, 2, 2, 10, 512)
        .transpose(3, 4, 5, 0, 2, 1, 6, 7)
        .reshape(2, 2, 2, cols, 512)
    )
    kernel2 = conv2_weight.transpose(0, 1, 2, 4, 3).reshape(27 * 32, 512)
    held, to_above, to_below = run(
        cache_conv,
        [((128, cols), F32), ((64, cols), F32), ((64, cols), F32)],
        (images, kernel2),
        "cache_conv",
        16,
    )
    from_above = lax.ppermute(to_below, space, down)
    from_below = lax.ppermute(to_above, space, up)
    out = run(
        functools.partial(up_conv, sizes=sizes),
        ((16, cols // 16, 128), BF16),
        (
            stats2,
            gathered,
            row_above,
            row_below,
            norm2_gain[None],
            norm2_bias[None],
            kernel2,
            held,
            from_above,
            from_below,
            conv2_bias[None],
        ),
        "up_conv",
        16,
    )
    out = lax.all_to_all(out, ("x", "h", "k"), 0, 0, tiled=True)
    out = out.reshape(16, 10, 2, 2, 32).transpose(2, 1, 3, 0, 4)
    return out.reshape(1, 2, 20, 512)


def solution(mesh):
    peers = mesh.shape["space"]
    n_l = 8 if peers % 8 == 0 else 2
    n_y = peers // n_l
    fine = Mesh(mesh.devices.reshape(n_y, n_l, 4, 2, 2), ("y", "l", "x", "h", "k"))
    space, chan = ("y", "l"), ("x", "h", "k")
    placed = (
        P(None, space, None, chan),
        P(None, space, None, chan),
        P(chan),
        P(chan),
        P(None, None, None, chan, None),
        P(chan),
        P(None, space, chan, None),
        P(),
        P(),
        P(None, None, None, None, chan),
        P(),
    )
    return jax.shard_map(
        functools.partial(on_device, (n_y, n_l)),
        mesh=fine,
        in_specs=placed,
        out_specs=P(None, space, chan, None),
        check_vma=False,
    )
```

```python
import functools

import jax
import jax.numpy as jnp
from jax import lax
from jax.experimental import pallas as pl
from jax.experimental.pallas import tpu as pltpu
from jax.sharding import Mesh
from jax.sharding import PartitionSpec as P


GS = 16
EPS = 1e-06
F32 = jnp.float32
BF16 = jnp.bfloat16
USE_KERNELS = True
FIRST_GRANT = 56


def run(fn, out_shapes, args, grant=8, late=()):
    if not USE_KERNELS:
        return fn(*[(lambda a=a: a) if i in late else a for i, a in enumerate(args)])
    n_a, single = len(args), isinstance(out_shapes, tuple)
    shapes = [out_shapes] if single else list(out_shapes)
    n_o = len(shapes)

    def body(*refs):
        held = refs[n_a + n_o :]
        ins = [None if i in late else r[...] for i, r in enumerate(refs[:n_a])]
        for spot, i in enumerate(late):
            copy = pltpu.make_async_copy(refs[i], held[2 * spot], held[2 * spot + 1])
            copy.start()

            def ready(copy=copy, buffer=held[2 * spot]):
                copy.wait()
                return buffer[...]

            ins[i] = ready
        outs = fn(*ins)
        outs = [outs] if single else outs
        for ref, value in zip(refs[n_a : n_a + n_o], outs):
            ref[...] = value

    vmem = pl.BlockSpec(memory_space=pltpu.VMEM)
    far = pl.BlockSpec(memory_space=pltpu.HBM)
    scratch = []
    for i in late:
        scratch += [pltpu.VMEM(args[i].shape, args[i].dtype), pltpu.SemaphoreType.DMA]
    res = pl.pallas_call(
        body,
        out_shape=[jax.ShapeDtypeStruct(s, d) for s, d in shapes],
        in_specs=[far if i in late else vmem for i in range(n_a)],
        out_specs=[vmem] * n_o,
        scratch_shapes=scratch,
        compiler_params=pltpu.CompilerParams(vmem_limit_bytes=grant << 20),
    )(*args)
    return res[0] if single else res


def to_row(col):
    n = col.shape[0]
    eye = lax.broadcasted_iota(jnp.int32, (n, n), 0) == lax.broadcasted_iota(jnp.int32, (n, n), 1)
    return jnp.sum(jnp.where(eye, col, 0.0), axis=0, keepdims=True)


def to_col(row, repeat):
    n = row.shape[1]
    rows = lax.broadcasted_iota(jnp.int32, (n * repeat, n), 0)
    lanes = lax.broadcasted_iota(jnp.int32, (n * repeat, n), 1)
    pick = (rows >= lanes * repeat) & (rows < lanes * repeat + repeat)
    return jnp.sum(jnp.where(pick, row, 0.0), axis=1, keepdims=True)


def partial_stats(values, peers):
    rows, cols = values.shape
    groups = rows // GS
    x = values.astype(F32)
    mean = jnp.sum(jnp.sum(x, axis=1, keepdims=True).reshape(groups, GS, 1), axis=1) / (GS * cols)
    dev = x.reshape(groups, GS, cols) - mean[:, :, None]
    sq = jnp.sum(jnp.sum(dev * dev, axis=2, keepdims=True), axis=1)
    row = jnp.concatenate(
        [to_row(mean), to_row(sq), jnp.zeros((1, 128 - 2 * groups), F32)], axis=1
    )
    return jnp.broadcast_to(row[None], (peers, 1, 128))


def merge_stats(parts, groups, count):
    peers = parts.shape[0]
    means = parts[:, 0, :groups]
    sq = parts[:, 0, groups : 2 * groups]
    mean = jnp.sum(means, axis=0, keepdims=True) / peers
    gap = means - mean
    var = (jnp.sum(sq, axis=0, keepdims=True) + count * jnp.sum(gap * gap, axis=0, keepdims=True)) / (
        count * peers
    )
    return mean, lax.rsqrt(var + EPS)


def norm_silu(x, mean, scale, gain, bias):
    v = (x.astype(F32) - mean) * scale * gain + bias
    low = v < -80.0
    e = jnp.exp(jnp.where(low, v, -v))
    return jnp.where(low, v * e, v / (1.0 + jnp.where(low, 0.0, e)))


def wide_col(row):
    n = row.shape[1]
    return jnp.concatenate([to_col(row[:, i : i + 128], 1) for i in range(0, n, 128)], axis=0)


def pack(a):
    tail = jnp.concatenate([a[16 * i : 16 * i + 16, 128:] for i in range(4)], axis=1)
    return jnp.concatenate([a[:, :128], tail], axis=0)


def unpack(a):
    tail = jnp.concatenate([a[64:, 32 * i : 32 * i + 32] for i in range(4)], axis=0)
    return jnp.concatenate([a[:64], tail], axis=1)


def right(a):
    return jnp.concatenate([jnp.zeros((a.shape[0], 1), a.dtype), a[:, :-1]], axis=1)


def left(a):
    return jnp.concatenate([a[:, 1:], jnp.zeros((a.shape[0], 1), a.dtype)], axis=1)


def edges(sizes):
    n_y, n_l = sizes
    row = lax.axis_index("y") * n_l + lax.axis_index("l")
    return row > 0, row < n_y * n_l - 1


def first_pass(own, cache, gain, bias, late_bias, peers):
    cols = jnp.concatenate([to_col(v, 1) for v in (gain, bias, late_bias)], axis=1)
    return partial_stats(own, peers), jnp.concatenate([cache, own[None]], axis=0), cols


def mid_conv(parts, raw, above, below, affine, kernel, sizes):
    chans, cols = raw.shape[1:]
    groups = chans // GS
    mean, scale = merge_stats(parts, groups, GS * cols)
    mean, scale = to_col(mean, GS), to_col(scale, GS)
    gain, bias = affine[:, :1], affine[:, 1:2]
    has = edges(sizes)
    pieces = []
    for t in range(3):
        for dy, src in enumerate((above, raw, below)):
            x = src[t].astype(F32)
            if t == 2:
                x = norm_silu(x, mean, scale, gain, bias)
                if dy != 1:
                    x = jnp.where(has[0 if dy == 0 else 1], x, 0.0)
            pieces += [right(x).astype(BF16), x.astype(BF16), left(x).astype(BF16)]
    columns = jnp.concatenate(pieces, axis=0)
    out = jnp.dot(columns.T, kernel(), preferred_element_type=F32).T
    blocks = []
    for x in range(4):
        for k in range(2):
            both = [out[(x * 4 + h * 2 + k) * 32 :][:32] for h in range(2)]
            blocks.append(pack(jnp.concatenate(both, axis=0)))
    return jnp.stack(blocks)


def fold(parts, own, affine):
    total = unpack(jnp.sum(parts, axis=0))
    extra = own.astype(F32) + affine[:, 2:3]
    zero = jnp.zeros_like(extra)
    first = lax.axis_index("h") == 0
    return pack(
        total
        + jnp.concatenate([jnp.where(first, extra, zero), jnp.where(first, zero, extra)], axis=0)
    )


def merge(mine, other):
    merged = (mine + other).astype(BF16)
    return jnp.broadcast_to(merged[None], (8,) + merged.shape)


def rows_of(gathered):
    blocks = [unpack(gathered[i].astype(F32)) for i in range(8)]
    return jnp.concatenate(
        [
            blocks[x * 2 + k][h * 32 : (h + 1) * 32]
            for x in range(4)
            for h in range(2)
            for k in range(2)
        ],
        axis=0,
    )


def row_stats(gathered, peers):
    return partial_stats(rows_of(gathered), peers)


def taps(prod):
    return [[prod[(dy * 3 + dx) * 32 : (dy * 3 + dx + 1) * 32] for dx in range(3)] for dy in range(3)]


def cache_conv(images, kernel):
    per = 9 * 32
    sums = {}

    def add(key, value):
        sums[key] = sums[key] + value if key in sums else value

    for t in range(2):
        w = kernel[t * per : (t + 1) * per]
        for r in range(2):
            even, odd = (
                taps(
                    lax.dot_general(
                        w, images[t, r, p], (((1,), (1,)), ((), ())), preferred_element_type=F32
                    )
                )
                for p in range(2)
            )
            for dy in range(3):
                o = r + 1 - dy
                add((o, "m", 0), even[dy][1] + odd[dy][2])
                add((o, "r", 0), odd[dy][0])
                add((o, "m", 1), even[dy][0] + odd[dy][1])
                add((o, "l", 1), even[dy][2])

    def out(o):
        return jnp.concatenate(
            [
                sums[(o, "m", 0)] + right(sums[(o, "r", 0)]),
                sums[(o, "m", 1)] + left(sums[(o, "l", 1)]),
            ],
            axis=0,
        )

    return jnp.concatenate([out(0), out(1)], axis=0), out(-1), out(2)


def up_columns(gain, bias, out_bias):
    chan = lax.axis_index("x") * 4 + lax.axis_index("h") * 2 + lax.axis_index("k")
    rows = lax.broadcasted_iota(jnp.int32, (32, out_bias.shape[1]), 0)
    lanes = lax.broadcasted_iota(jnp.int32, (32, out_bias.shape[1]), 1)
    picked = jnp.sum(jnp.where(lanes == rows + chan * 32, out_bias, 0.0), axis=1, keepdims=True)
    return jnp.concatenate([wide_col(gain), wide_col(bias)], axis=1), jnp.concatenate(
        [picked] * 4, axis=0
    )


def up_weights(kernel):
    return jnp.concatenate(
        [kernel[(18 + dy * 3) * 32 : (21 + dy * 3) * 32] for dy in range(3)], axis=1
    )


def up_conv(parts, row, above, below, affine, lhs, held, from_above, from_below, out_bias, sizes):
    row, above, below = rows_of(row), rows_of(above), rows_of(below)
    chans, cols = row.shape
    groups = chans // GS
    mean, scale = merge_stats(parts, groups, GS * cols)
    mean, scale = to_col(mean, GS), to_col(scale, GS)
    gain, bias = affine[:, :1], affine[:, 1:2]
    has = edges(sizes)

    def image(x, keep=None):
        v = norm_silu(x, mean, scale, gain, bias)
        if keep is not None:
            v = jnp.where(keep, v, 0.0)
        return v.astype(BF16)

    here = image(row)
    outs = []
    for images in ((image(above, has[0]), here, here), (here, here, image(below, has[1]))):
        prod = jnp.dot(lhs, jnp.concatenate(images, axis=0), preferred_element_type=F32)
        cut = [prod[dx * 32 : (dx + 1) * 32] for dx in range(3)]
        outs += [right(cut[0]) + cut[1] + cut[2], cut[0] + cut[1] + left(cut[2])]
    total = jnp.concatenate(outs, axis=0) + held
    total = total + jnp.concatenate([from_above, from_below], axis=0)
    total = (total + out_bias).T
    part = cols // 16
    return jnp.stack([total[c * part : (c + 1) * part] for c in range(16)]).astype(BF16)


def on_device(
    sizes,
    latent,
    cache_mid,
    norm1_gain,
    norm1_bias,
    conv1_weight,
    conv1_bias,
    cache_up,
    norm2_gain,
    norm2_bias,
    conv2_weight,
    conv2_bias,
):
    n_y, n_l = sizes
    peers = n_y * n_l
    cols, chans = latent.shape[2], latent.shape[3]
    sizes = (n_y, n_l)
    hi = lax.axis_index("h")
    space = ("y", "l")
    own = latent[0, 0].T
    stats, raw, affine = run(
        functools.partial(first_pass, peers=peers),
        [((peers, 1, 128), F32), ((3, chans, cols), BF16), ((chans, 3), F32)],
        (own, cache_mid[:, 0].transpose(0, 2, 1), norm1_gain[None], norm1_bias[None], conv1_bias[None]),
        FIRST_GRANT,
    )
    stats = lax.all_to_all(stats, space, 0, 0, tiled=True)
    down = [(i, i + 1) for i in range(peers - 1)]
    up = [(i + 1, i) for i in range(peers - 1)]
    above = lax.ppermute(raw, space, down)
    below = lax.ppermute(raw, space, up)
    partial = run(
        functools.partial(mid_conv, sizes=sizes),
        ((8, 80, 128), F32),
        (stats, raw, above, below, affine, conv1_weight.reshape(27 * chans, 512)),
        FIRST_GRANT,
        late=(5,),
    )
    partial = lax.all_to_all(partial, ("x", "k"), 0, 0, tiled=True)
    mine = run(fold, ((80, 128), F32), (partial, own, affine))
    other = lax.ppermute(mine, "h", [(0, 1), (1, 0)])
    gathered = run(merge, ((8, 80, 128), BF16), (mine, other))
    gathered = lax.all_to_all(gathered, ("x", "k"), 0, 0, tiled=True)
    stats2 = run(functools.partial(row_stats, peers=peers), ((peers, 1, 128), F32), (gathered,))
    stats2 = lax.all_to_all(stats2, space, 0, 0, tiled=True)

    def at(y, l, h):
        return (y * n_l + l) * 2 + h

    down_h, up_h = [], []
    for y in range(n_y):
        for l in range(n_l):
            for h in range(2):
                if l < n_l - 1:
                    pair = (at(y, l, h), at(y, l + 1, h))
                elif y < n_y - 1:
                    pair = (at(y, l, h), at(y + 1, 0, 1 - h))
                else:
                    continue
                down_h.append(pair)
                up_h.append(pair[::-1])
    row_above = lax.ppermute(gathered, ("y", "l", "h"), down_h)
    row_below = lax.ppermute(gathered, ("y", "l", "h"), up_h)

    tile = cache_up.reshape(2, 2, 10, 2, 512).transpose(0, 1, 3, 2, 4)
    swapped = lax.ppermute(tile, "h", [(0, 1), (1, 0)])
    pair = jnp.where(hi == 0, jnp.stack([tile, swapped]), jnp.stack([swapped, tile]))
    copies = jnp.broadcast_to(pair[None], (8,) + pair.shape)
    spread = lax.all_to_all(copies, ("x", "k"), 0, 0, tiled=True)
    images = (
        spread.reshape(4, 2, 2, 2, 2, 2, 10, 512)
        .transpose(3, 4, 5, 0, 2, 1, 6, 7)
        .reshape(2, 2, 2, cols, 512)
    )
    kernel2 = conv2_weight.transpose(0, 1, 2, 4, 3).reshape(27 * 32, 512)
    held, to_above, to_below = run(
        cache_conv,
        [((128, cols), F32), ((64, cols), F32), ((64, cols), F32)],
        (images, kernel2),
        16,
    )
    from_above = lax.ppermute(to_below, space, down)
    from_below = lax.ppermute(to_above, space, up)
    affine2, bias_here = run(
        up_columns,
        [((512, 2), F32), ((128, 1), F32)],
        (norm2_gain[None], norm2_bias[None], conv2_bias[None]),
    )
    lhs = run(up_weights, ((3 * 32, 3 * 512), BF16), (kernel2,))
    out = run(
        functools.partial(up_conv, sizes=sizes),
        ((16, cols // 16, 128), BF16),
        (
            stats2,
            gathered,
            row_above,
            row_below,
            affine2,
            lhs,
            held,
            from_above,
            from_below,
            bias_here,
        ),
        16,
    )
    out = lax.all_to_all(out, ("x", "h", "k"), 0, 0, tiled=True)
    out = out.reshape(16, 10, 2, 2, 32).transpose(2, 1, 3, 0, 4)
    return out.reshape(1, 2, 20, 512)


def solution(mesh):
    peers = mesh.shape["space"]
    n_l = 8 if peers % 8 == 0 else 2
    n_y = peers // n_l
    fine = Mesh(mesh.devices.reshape(n_y, n_l, 4, 2, 2), ("y", "l", "x", "h", "k"))
    space, chan = ("y", "l"), ("x", "h", "k")
    placed = (
        P(None, space, None, chan),
        P(None, space, None, chan),
        P(chan),
        P(chan),
        P(None, None, None, chan, None),
        P(chan),
        P(None, space, chan, None),
        P(),
        P(),
        P(None, None, None, None, chan),
        P(),
    )

    def body(*args):
        return on_device((n_y, n_l), *args)

    return jax.shard_map(
        body,
        mesh=fine,
        in_specs=placed,
        out_specs=P(None, space, chan, None),
        check_vma=False,
    )
```

```python
import functools

import jax
import jax.numpy as jnp
from jax import lax
from jax.experimental import pallas as pl
from jax.experimental.pallas import tpu as pltpu
from jax.sharding import Mesh
from jax.sharding import PartitionSpec as P


GS = 16
EPS = 1e-06
F32 = jnp.float32
BF16 = jnp.bfloat16
USE_KERNELS = True
FIRST_GRANT = 56


def run(fn, out_shapes, args, grant=8, late=()):
    if not USE_KERNELS:
        return fn(*[(lambda a=a: a) if i in late else a for i, a in enumerate(args)])
    n_a, single = len(args), isinstance(out_shapes, tuple)
    shapes = [out_shapes] if single else list(out_shapes)
    n_o = len(shapes)

    def body(*refs):
        held = refs[n_a + n_o :]
        ins = [None if i in late else r[...] for i, r in enumerate(refs[:n_a])]
        for spot, i in enumerate(late):
            copy = pltpu.make_async_copy(refs[i], held[2 * spot], held[2 * spot + 1])
            copy.start()

            def ready(copy=copy, buffer=held[2 * spot]):
                copy.wait()
                return buffer[...]

            ins[i] = ready
        outs = fn(*ins)
        outs = [outs] if single else outs
        for ref, value in zip(refs[n_a : n_a + n_o], outs):
            ref[...] = value

    vmem = pl.BlockSpec(memory_space=pltpu.VMEM)
    far = pl.BlockSpec(memory_space=pltpu.HBM)
    scratch = []
    for i in late:
        scratch += [pltpu.VMEM(args[i].shape, args[i].dtype), pltpu.SemaphoreType.DMA]
    res = pl.pallas_call(
        body,
        out_shape=[jax.ShapeDtypeStruct(s, d) for s, d in shapes],
        in_specs=[far if i in late else vmem for i in range(n_a)],
        out_specs=[vmem] * n_o,
        scratch_shapes=scratch,
        compiler_params=pltpu.CompilerParams(vmem_limit_bytes=grant << 20),
    )(*args)
    return res[0] if single else res


def to_row(col):
    n = col.shape[0]
    eye = lax.broadcasted_iota(jnp.int32, (n, n), 0) == lax.broadcasted_iota(jnp.int32, (n, n), 1)
    return jnp.sum(jnp.where(eye, col, 0.0), axis=0, keepdims=True)


def to_col(row, repeat):
    n = row.shape[1]
    rows = lax.broadcasted_iota(jnp.int32, (n * repeat, n), 0)
    lanes = lax.broadcasted_iota(jnp.int32, (n * repeat, n), 1)
    pick = (rows >= lanes * repeat) & (rows < lanes * repeat + repeat)
    return jnp.sum(jnp.where(pick, row, 0.0), axis=1, keepdims=True)


def partial_stats(values, peers):
    rows, cols = values.shape
    groups = rows // GS
    x = values.astype(F32)
    mean = jnp.sum(jnp.sum(x, axis=1, keepdims=True).reshape(groups, GS, 1), axis=1) / (GS * cols)
    dev = x.reshape(groups, GS, cols) - mean[:, :, None]
    sq = jnp.sum(jnp.sum(dev * dev, axis=2, keepdims=True), axis=1)
    row = jnp.concatenate(
        [to_row(mean), to_row(sq), jnp.zeros((1, 128 - 2 * groups), F32)], axis=1
    )
    return jnp.broadcast_to(row[None], (peers, 1, 128))


def merge_stats(parts, groups, count):
    peers = parts.shape[0]
    means = parts[:, 0, :groups]
    sq = parts[:, 0, groups : 2 * groups]
    mean = jnp.sum(means, axis=0, keepdims=True) / peers
    gap = means - mean
    var = (jnp.sum(sq, axis=0, keepdims=True) + count * jnp.sum(gap * gap, axis=0, keepdims=True)) / (
        count * peers
    )
    return mean, lax.rsqrt(var + EPS)


def norm_silu(x, mean, scale, gain, bias):
    v = (x.astype(F32) - mean) * scale * gain + bias
    low = v < -80.0
    e = jnp.exp(jnp.where(low, v, -v))
    return jnp.where(low, v * e, v / (1.0 + jnp.where(low, 0.0, e)))


def wide_col(row):
    n = row.shape[1]
    return jnp.concatenate([to_col(row[:, i : i + 128], 1) for i in range(0, n, 128)], axis=0)


def pack(a):
    tail = jnp.concatenate([a[16 * i : 16 * i + 16, 128:] for i in range(4)], axis=1)
    return jnp.concatenate([a[:, :128], tail], axis=0)


def unpack(a):
    tail = jnp.concatenate([a[64:, 32 * i : 32 * i + 32] for i in range(4)], axis=0)
    return jnp.concatenate([a[:64], tail], axis=1)


def right(a):
    return jnp.concatenate([jnp.zeros((a.shape[0], 1), a.dtype), a[:, :-1]], axis=1)


def left(a):
    return jnp.concatenate([a[:, 1:], jnp.zeros((a.shape[0], 1), a.dtype)], axis=1)


def edges(sizes):
    n_y, n_l = sizes
    row = lax.axis_index("y") * n_l + lax.axis_index("l")
    return row > 0, row < n_y * n_l - 1


def first_pass(own, cache, gain, bias, late_bias, peers):
    cols = jnp.concatenate([to_col(v, 1) for v in (gain, bias, late_bias)], axis=1)
    return partial_stats(own, peers), jnp.concatenate([cache, own[None]], axis=0), cols


def mid_conv(parts, raw, above, below, affine, kernel, sizes):
    chans, cols = raw.shape[1:]
    groups = chans // GS
    mean, scale = merge_stats(parts, groups, GS * cols)
    mean, scale = to_col(mean, GS), to_col(scale, GS)
    gain, bias = affine[:, :1], affine[:, 1:2]
    has = edges(sizes)
    pieces = []
    for t in range(3):
        for dy, src in enumerate((above, raw, below)):
            x = src[t].astype(F32)
            if t == 2:
                x = norm_silu(x, mean, scale, gain, bias)
                if dy != 1:
                    x = jnp.where(has[0 if dy == 0 else 1], x, 0.0)
            pieces += [right(x).astype(BF16), x.astype(BF16), left(x).astype(BF16)]
    columns = jnp.concatenate(pieces, axis=0)
    out = jnp.dot(columns.T, kernel(), preferred_element_type=F32).T
    blocks = []
    for x in range(4):
        for k in range(2):
            both = [out[(x * 4 + h * 2 + k) * 32 :][:32] for h in range(2)]
            blocks.append(pack(jnp.concatenate(both, axis=0)))
    return jnp.stack(blocks)


def fold(parts, own, affine):
    total = unpack(jnp.sum(parts, axis=0))
    extra = own.astype(F32) + affine[:, 2:3]
    zero = jnp.zeros_like(extra)
    first = lax.axis_index("h") == 0
    return pack(
        total
        + jnp.concatenate([jnp.where(first, extra, zero), jnp.where(first, zero, extra)], axis=0)
    )


def merge(mine, other):
    merged = (mine + other).astype(BF16)
    return jnp.broadcast_to(merged[None], (8,) + merged.shape)


def rows_of(gathered):
    blocks = [unpack(gathered[i].astype(F32)) for i in range(8)]
    return jnp.concatenate(
        [
            blocks[x * 2 + k][h * 32 : (h + 1) * 32]
            for x in range(4)
            for h in range(2)
            for k in range(2)
        ],
        axis=0,
    )


def row_stats(gathered, peers):
    return partial_stats(rows_of(gathered), peers)


def taps(prod):
    return [[prod[(dy * 3 + dx) * 32 : (dy * 3 + dx + 1) * 32] for dx in range(3)] for dy in range(3)]


def cache_conv(images, kernel):
    per = 9 * 32
    sums = {}

    def add(key, value):
        sums[key] = sums[key] + value if key in sums else value

    for t in range(2):
        w = kernel[t * per : (t + 1) * per]
        for r in range(2):
            even, odd = (
                taps(
                    lax.dot_general(
                        w, images[t, r, p], (((1,), (1,)), ((), ())), preferred_element_type=F32
                    )
                )
                for p in range(2)
            )
            for dy in range(3):
                o = r + 1 - dy
                add((o, "m", 0), even[dy][1] + odd[dy][2])
                add((o, "r", 0), odd[dy][0])
                add((o, "m", 1), even[dy][0] + odd[dy][1])
                add((o, "l", 1), even[dy][2])

    def out(o):
        return jnp.concatenate(
            [
                sums[(o, "m", 0)] + right(sums[(o, "r", 0)]),
                sums[(o, "m", 1)] + left(sums[(o, "l", 1)]),
            ],
            axis=0,
        )

    return jnp.concatenate([out(0), out(1)], axis=0), out(-1), out(2)


def assemble(*came):
    x = lax.axis_index("x")
    out = []
    for i in range(4):
        block = came[(3 - i) % 4]
        for here in range(3):
            block = jnp.where(x == here, came[(here - i) % 4], block)
        out.append(block)
    return jnp.stack(out)


def up_columns(gain, bias, out_bias):
    chan = lax.axis_index("x") * 4 + lax.axis_index("h") * 2 + lax.axis_index("k")
    rows = lax.broadcasted_iota(jnp.int32, (32, out_bias.shape[1]), 0)
    lanes = lax.broadcasted_iota(jnp.int32, (32, out_bias.shape[1]), 1)
    picked = jnp.sum(jnp.where(lanes == rows + chan * 32, out_bias, 0.0), axis=1, keepdims=True)
    return jnp.concatenate([wide_col(gain), wide_col(bias)], axis=1), jnp.concatenate(
        [picked] * 4, axis=0
    )


def up_weights(kernel):
    return jnp.concatenate(
        [kernel[(18 + dy * 3) * 32 : (21 + dy * 3) * 32] for dy in range(3)], axis=1
    )


def up_conv(parts, row, above, below, affine, lhs, held, from_above, from_below, out_bias, sizes):
    row, above, below = rows_of(row), rows_of(above), rows_of(below)
    chans, cols = row.shape
    groups = chans // GS
    mean, scale = merge_stats(parts, groups, GS * cols)
    mean, scale = to_col(mean, GS), to_col(scale, GS)
    gain, bias = affine[:, :1], affine[:, 1:2]
    has = edges(sizes)

    def image(x, keep=None):
        v = norm_silu(x, mean, scale, gain, bias)
        if keep is not None:
            v = jnp.where(keep, v, 0.0)
        return v.astype(BF16)

    here = image(row)
    outs = []
    for images in ((image(above, has[0]), here, here), (here, here, image(below, has[1]))):
        prod = jnp.dot(lhs, jnp.concatenate(images, axis=0), preferred_element_type=F32)
        cut = [prod[dx * 32 : (dx + 1) * 32] for dx in range(3)]
        outs += [right(cut[0]) + cut[1] + cut[2], cut[0] + cut[1] + left(cut[2])]
    total = jnp.concatenate(outs, axis=0) + held
    total = total + jnp.concatenate([from_above, from_below], axis=0)
    total = (total + out_bias).T
    part = cols // 16
    return jnp.stack([total[c * part : (c + 1) * part] for c in range(16)]).astype(BF16)


def on_device(
    sizes,
    latent,
    cache_mid,
    norm1_gain,
    norm1_bias,
    conv1_weight,
    conv1_bias,
    cache_up,
    norm2_gain,
    norm2_bias,
    conv2_weight,
    conv2_bias,
):
    n_y, n_l = sizes
    peers = n_y * n_l
    cols, chans = latent.shape[2], latent.shape[3]
    sizes = (n_y, n_l)
    hi = lax.axis_index("h")
    space = ("y", "l")
    own = latent[0, 0].T
    stats, raw, affine = run(
        functools.partial(first_pass, peers=peers),
        [((peers, 1, 128), F32), ((3, chans, cols), BF16), ((chans, 3), F32)],
        (own, cache_mid[:, 0].transpose(0, 2, 1), norm1_gain[None], norm1_bias[None], conv1_bias[None]),
        FIRST_GRANT,
    )
    stats = lax.all_to_all(stats, space, 0, 0, tiled=True)
    down = [(i, i + 1) for i in range(peers - 1)]
    up = [(i + 1, i) for i in range(peers - 1)]
    above = lax.ppermute(raw, space, down)
    below = lax.ppermute(raw, space, up)
    partial = run(
        functools.partial(mid_conv, sizes=sizes),
        ((8, 80, 128), F32),
        (stats, raw, above, below, affine, conv1_weight.reshape(27 * chans, 512)),
        FIRST_GRANT,
        late=(5,),
    )
    partial = lax.all_to_all(partial, ("x", "k"), 0, 0, tiled=True)
    mine = run(fold, ((80, 128), F32), (partial, own, affine))
    other = lax.ppermute(mine, "h", [(0, 1), (1, 0)])
    gathered = run(merge, ((8, 80, 128), BF16), (mine, other))
    gathered = lax.all_to_all(gathered, ("x", "k"), 0, 0, tiled=True)
    stats2 = run(functools.partial(row_stats, peers=peers), ((peers, 1, 128), F32), (gathered,))
    stats2 = lax.all_to_all(stats2, space, 0, 0, tiled=True)

    def at(y, l, h):
        return (y * n_l + l) * 2 + h

    down_h, up_h = [], []
    for y in range(n_y):
        for l in range(n_l):
            for h in range(2):
                if l < n_l - 1:
                    pair = (at(y, l, h), at(y, l + 1, h))
                elif y < n_y - 1:
                    pair = (at(y, l, h), at(y + 1, 0, 1 - h))
                else:
                    continue
                down_h.append(pair)
                up_h.append(pair[::-1])
    row_above = lax.ppermute(gathered, ("y", "l", "h"), down_h)
    row_below = lax.ppermute(gathered, ("y", "l", "h"), up_h)

    tile = cache_up.reshape(2, 2, 10, 2, 512).transpose(0, 1, 3, 2, 4)
    swapped = lax.ppermute(tile, "h", [(0, 1), (1, 0)])
    pair = jnp.where(hi == 0, jnp.stack([tile, swapped]), jnp.stack([swapped, tile]))
    came = [pair] + [
        lax.ppermute(pair, "x", [(i, (i + d) % 4) for i in range(4)]) for d in range(1, 4)
    ]
    mine_k = run(assemble, ((4,) + pair.shape, BF16), came)
    other_k = lax.ppermute(mine_k, "k", [(0, 1), (1, 0)])
    core = lax.axis_index("k")
    both = jnp.where(core == 0, jnp.stack([mine_k, other_k]), jnp.stack([other_k, mine_k]))
    images = both.transpose(3, 4, 5, 1, 2, 0, 6, 7).reshape(2, 2, 2, cols, 512)
    kernel2 = conv2_weight.transpose(0, 1, 2, 4, 3).reshape(27 * 32, 512)
    held, to_above, to_below = run(
        cache_conv,
        [((128, cols), F32), ((64, cols), F32), ((64, cols), F32)],
        (images, kernel2),
        16,
    )
    from_above = lax.ppermute(to_below, space, down)
    from_below = lax.ppermute(to_above, space, up)
    affine2, bias_here = run(
        up_columns,
        [((512, 2), F32), ((128, 1), F32)],
        (norm2_gain[None], norm2_bias[None], conv2_bias[None]),
    )
    lhs = run(up_weights, ((3 * 32, 3 * 512), BF16), (kernel2,))
    out = run(
        functools.partial(up_conv, sizes=sizes),
        ((16, cols // 16, 128), BF16),
        (
            stats2,
            gathered,
            row_above,
            row_below,
            affine2,
            lhs,
            held,
            from_above,
            from_below,
            bias_here,
        ),
        16,
    )
    out = lax.all_to_all(out, ("x", "h", "k"), 0, 0, tiled=True)
    out = out.reshape(16, 10, 2, 2, 32).transpose(2, 1, 3, 0, 4)
    return out.reshape(1, 2, 20, 512)


def solution(mesh):
    peers = mesh.shape["space"]
    n_l = 8 if peers % 8 == 0 else 2
    n_y = peers // n_l
    fine = Mesh(mesh.devices.reshape(n_y, n_l, 4, 2, 2), ("y", "l", "x", "h", "k"))
    space, chan = ("y", "l"), ("x", "h", "k")
    placed = (
        P(None, space, None, chan),
        P(None, space, None, chan),
        P(chan),
        P(chan),
        P(None, None, None, chan, None),
        P(chan),
        P(None, space, chan, None),
        P(),
        P(),
        P(None, None, None, None, chan),
        P(),
    )

    def body(*args):
        return on_device((n_y, n_l), *args)

    return jax.shard_map(
        body,
        mesh=fine,
        in_specs=placed,
        out_specs=P(None, space, chan, None),
        check_vma=False,
    )
```

```python
import functools

import jax
import jax.numpy as jnp
from jax import lax
from jax.experimental import pallas as pl
from jax.experimental.pallas import tpu as pltpu
from jax.sharding import Mesh
from jax.sharding import PartitionSpec as P


GS = 16
EPS = 1e-06
F32 = jnp.float32
BF16 = jnp.bfloat16
USE_KERNELS = True
FIRST_GRANT = 56


def run(fn, out_shapes, args, grant=8, late=()):
    if not USE_KERNELS:
        return fn(*[(lambda a=a: a) if i in late else a for i, a in enumerate(args)])
    n_a, single = len(args), isinstance(out_shapes, tuple)
    shapes = [out_shapes] if single else list(out_shapes)
    n_o = len(shapes)

    def body(*refs):
        held = refs[n_a + n_o :]
        ins = [None if i in late else r[...] for i, r in enumerate(refs[:n_a])]
        for spot, i in enumerate(late):
            copy = pltpu.make_async_copy(refs[i], held[2 * spot], held[2 * spot + 1])
            copy.start()

            def ready(copy=copy, buffer=held[2 * spot]):
                copy.wait()
                return buffer[...]

            ins[i] = ready
        outs = fn(*ins)
        outs = [outs] if single else outs
        for ref, value in zip(refs[n_a : n_a + n_o], outs):
            ref[...] = value

    vmem = pl.BlockSpec(memory_space=pltpu.VMEM)
    far = pl.BlockSpec(memory_space=pltpu.HBM)
    scratch = []
    for i in late:
        scratch += [pltpu.VMEM(args[i].shape, args[i].dtype), pltpu.SemaphoreType.DMA]
    res = pl.pallas_call(
        body,
        out_shape=[jax.ShapeDtypeStruct(s, d) for s, d in shapes],
        in_specs=[far if i in late else vmem for i in range(n_a)],
        out_specs=[vmem] * n_o,
        scratch_shapes=scratch,
        compiler_params=pltpu.CompilerParams(vmem_limit_bytes=grant << 20),
    )(*args)
    return res[0] if single else res


def to_row(col):
    n = col.shape[0]
    eye = lax.broadcasted_iota(jnp.int32, (n, n), 0) == lax.broadcasted_iota(jnp.int32, (n, n), 1)
    return jnp.sum(jnp.where(eye, col, 0.0), axis=0, keepdims=True)


def to_col(row, repeat):
    n = row.shape[1]
    rows = lax.broadcasted_iota(jnp.int32, (n * repeat, n), 0)
    lanes = lax.broadcasted_iota(jnp.int32, (n * repeat, n), 1)
    pick = (rows >= lanes * repeat) & (rows < lanes * repeat + repeat)
    return jnp.sum(jnp.where(pick, row, 0.0), axis=1, keepdims=True)


def partial_stats(values, peers):
    rows, cols = values.shape
    groups = rows // GS
    x = values.astype(F32)
    mean = jnp.sum(jnp.sum(x, axis=1, keepdims=True).reshape(groups, GS, 1), axis=1) / (GS * cols)
    dev = x.reshape(groups, GS, cols) - mean[:, :, None]
    sq = jnp.sum(jnp.sum(dev * dev, axis=2, keepdims=True), axis=1)
    row = jnp.concatenate(
        [to_row(mean), to_row(sq), jnp.zeros((1, 128 - 2 * groups), F32)], axis=1
    )
    return jnp.broadcast_to(row[None], (peers, 1, 128))


def merge_stats(parts, groups, count):
    peers = parts.shape[0]
    means = parts[:, 0, :groups]
    sq = parts[:, 0, groups : 2 * groups]
    mean = jnp.sum(means, axis=0, keepdims=True) / peers
    gap = means - mean
    var = (jnp.sum(sq, axis=0, keepdims=True) + count * jnp.sum(gap * gap, axis=0, keepdims=True)) / (
        count * peers
    )
    return mean, lax.rsqrt(var + EPS)


def norm_silu(x, mean, scale, gain, bias):
    v = (x.astype(F32) - mean) * scale * gain + bias
    low = v < -80.0
    e = jnp.exp(jnp.where(low, v, -v))
    return jnp.where(low, v * e, v / (1.0 + jnp.where(low, 0.0, e)))


def wide_col(row):
    n = row.shape[1]
    return jnp.concatenate([to_col(row[:, i : i + 128], 1) for i in range(0, n, 128)], axis=0)


def pack(a):
    tail = jnp.concatenate([a[16 * i : 16 * i + 16, 128:] for i in range(4)], axis=1)
    return jnp.concatenate([a[:, :128], tail], axis=0)


def unpack(a):
    tail = jnp.concatenate([a[64:, 32 * i : 32 * i + 32] for i in range(4)], axis=0)
    return jnp.concatenate([a[:64], tail], axis=1)


def right(a):
    return jnp.concatenate([jnp.zeros((a.shape[0], 1), a.dtype), a[:, :-1]], axis=1)


def left(a):
    return jnp.concatenate([a[:, 1:], jnp.zeros((a.shape[0], 1), a.dtype)], axis=1)


def edges(sizes):
    n_y, n_l = sizes
    row = lax.axis_index("y") * n_l + lax.axis_index("l")
    return row > 0, row < n_y * n_l - 1


def first_pass(own, cache, gain, bias, late_bias, peers):
    cols = jnp.concatenate([to_col(v, 1) for v in (gain, bias, late_bias)], axis=1)
    return partial_stats(own, peers), jnp.concatenate([cache, own[None]], axis=0), cols


def mid_conv(parts, raw, above, below, affine, kernel, sizes):
    chans, cols = raw.shape[1:]
    groups = chans // GS
    mean, scale = merge_stats(parts, groups, GS * cols)
    mean, scale = to_col(mean, GS), to_col(scale, GS)
    gain, bias = affine[:, :1], affine[:, 1:2]
    has = edges(sizes)
    pieces = []
    for t in range(3):
        for dy, src in enumerate((above, raw, below)):
            x = src[t].astype(F32)
            if t == 2:
                x = norm_silu(x, mean, scale, gain, bias)
                if dy != 1:
                    x = jnp.where(has[0 if dy == 0 else 1], x, 0.0)
            pieces += [right(x).astype(BF16), x.astype(BF16), left(x).astype(BF16)]
    columns = jnp.concatenate(pieces, axis=0)
    out = jnp.dot(columns.T, kernel(), preferred_element_type=F32).T
    blocks = []
    for x in range(4):
        for k in range(2):
            both = [out[(x * 4 + h * 2 + k) * 32 :][:32] for h in range(2)]
            blocks.append(pack(jnp.concatenate(both, axis=0)))
    return jnp.stack(blocks)


def fold(parts, own, affine):
    total = unpack(jnp.sum(parts, axis=0))
    extra = own.astype(F32) + affine[:, 2:3]
    zero = jnp.zeros_like(extra)
    first = lax.axis_index("h") == 0
    return pack(
        total
        + jnp.concatenate([jnp.where(first, extra, zero), jnp.where(first, zero, extra)], axis=0)
    )


def merge(mine, other):
    merged = (mine + other).astype(BF16)
    return jnp.broadcast_to(merged[None], (8,) + merged.shape)


def rows_of(gathered):
    blocks = [unpack(gathered[i].astype(F32)) for i in range(8)]
    return jnp.concatenate(
        [
            blocks[x * 2 + k][h * 32 : (h + 1) * 32]
            for x in range(4)
            for h in range(2)
            for k in range(2)
        ],
        axis=0,
    )


def row_stats(gathered, to_above, to_below, peers):
    return (
        partial_stats(rows_of(gathered), peers),
        jnp.concatenate([gathered, to_above], axis=0),
        jnp.concatenate([gathered, to_below], axis=0),
    )


def halves(a):
    a = pack(a)
    high = a.astype(BF16)
    return jnp.stack([high, (a - high.astype(F32)).astype(BF16)])


def whole(blocks):
    return unpack(blocks[0].astype(F32) + blocks[1].astype(F32))


def taps(prod):
    return [[prod[(dy * 3 + dx) * 32 : (dy * 3 + dx + 1) * 32] for dx in range(3)] for dy in range(3)]


def cache_conv(images, kernel):
    per = 9 * 32
    sums = {}

    def add(key, value):
        sums[key] = sums[key] + value if key in sums else value

    for t in range(2):
        w = kernel[t * per : (t + 1) * per]
        for r in range(2):
            even, odd = (
                taps(
                    lax.dot_general(
                        w, images[t, r, p], (((1,), (1,)), ((), ())), preferred_element_type=F32
                    )
                )
                for p in range(2)
            )
            for dy in range(3):
                o = r + 1 - dy
                add((o, "m", 0), even[dy][1] + odd[dy][2])
                add((o, "r", 0), odd[dy][0])
                add((o, "m", 1), even[dy][0] + odd[dy][1])
                add((o, "l", 1), even[dy][2])

    def out(o):
        return jnp.concatenate(
            [
                sums[(o, "m", 0)] + right(sums[(o, "r", 0)]),
                sums[(o, "m", 1)] + left(sums[(o, "l", 1)]),
            ],
            axis=0,
        )

    return jnp.concatenate([out(0), out(1)], axis=0), halves(out(-1)), halves(out(2))


def up_columns(gain, bias, out_bias):
    chan = lax.axis_index("x") * 4 + lax.axis_index("h") * 2 + lax.axis_index("k")
    rows = lax.broadcasted_iota(jnp.int32, (32, out_bias.shape[1]), 0)
    lanes = lax.broadcasted_iota(jnp.int32, (32, out_bias.shape[1]), 1)
    picked = jnp.sum(jnp.where(lanes == rows + chan * 32, out_bias, 0.0), axis=1, keepdims=True)
    return jnp.concatenate([wide_col(gain), wide_col(bias)], axis=1), jnp.concatenate(
        [picked] * 4, axis=0
    )


def up_weights(kernel):
    return jnp.concatenate(
        [kernel[(18 + dy * 3) * 32 : (21 + dy * 3) * 32] for dy in range(3)], axis=1
    )


def up_conv(parts, row, above, below, affine, lhs, held, out_bias, sizes):
    from_above, from_below = whole(above[8:]), whole(below[8:])
    row, above, below = rows_of(row), rows_of(above[:8]), rows_of(below[:8])
    chans, cols = row.shape
    groups = chans // GS
    mean, scale = merge_stats(parts, groups, GS * cols)
    mean, scale = to_col(mean, GS), to_col(scale, GS)
    gain, bias = affine[:, :1], affine[:, 1:2]
    has = edges(sizes)

    def image(x, keep=None):
        v = norm_silu(x, mean, scale, gain, bias)
        if keep is not None:
            v = jnp.where(keep, v, 0.0)
        return v.astype(BF16)

    here = image(row)
    outs = []
    for images in ((image(above, has[0]), here, here), (here, here, image(below, has[1]))):
        prod = jnp.dot(lhs, jnp.concatenate(images, axis=0), preferred_element_type=F32)
        cut = [prod[dx * 32 : (dx + 1) * 32] for dx in range(3)]
        outs += [right(cut[0]) + cut[1] + cut[2], cut[0] + cut[1] + left(cut[2])]
    total = jnp.concatenate(outs, axis=0) + held
    total = total + jnp.concatenate([from_above, from_below], axis=0)
    total = (total + out_bias).T
    part = cols // 16
    return jnp.stack([total[c * part : (c + 1) * part] for c in range(16)]).astype(BF16)


def on_device(
    sizes,
    latent,
    cache_mid,
    norm1_gain,
    norm1_bias,
    conv1_weight,
    conv1_bias,
    cache_up,
    norm2_gain,
    norm2_bias,
    conv2_weight,
    conv2_bias,
):
    n_y, n_l = sizes
    peers = n_y * n_l
    cols, chans = latent.shape[2], latent.shape[3]
    sizes = (n_y, n_l)
    space = ("y", "l")
    own = latent[0, 0].T
    stats, raw, affine = run(
        functools.partial(first_pass, peers=peers),
        [((peers, 1, 128), F32), ((3, chans, cols), BF16), ((chans, 3), F32)],
        (own, cache_mid[:, 0].transpose(0, 2, 1), norm1_gain[None], norm1_bias[None], conv1_bias[None]),
        FIRST_GRANT,
    )
    stats = lax.all_to_all(stats, space, 0, 0, tiled=True)
    down = [(i, i + 1) for i in range(peers - 1)]
    up = [(i + 1, i) for i in range(peers - 1)]
    above = lax.ppermute(raw, space, down)
    below = lax.ppermute(raw, space, up)
    partial = run(
        functools.partial(mid_conv, sizes=sizes),
        ((8, 80, 128), F32),
        (stats, raw, above, below, affine, conv1_weight.reshape(27 * chans, 512)),
        FIRST_GRANT,
        late=(5,),
    )
    partial = lax.all_to_all(partial, ("x", "k"), 0, 0, tiled=True)
    mine = run(fold, ((80, 128), F32), (partial, own, affine))
    other = lax.ppermute(mine, "h", [(0, 1), (1, 0)])
    gathered = run(merge, ((8, 80, 128), BF16), (mine, other))
    gathered = lax.all_to_all(gathered, ("x", "k"), 0, 0, tiled=True)
    tile = cache_up.reshape(2, 2, 10, 2, 512).transpose(0, 1, 3, 2, 4).reshape(80, 512)
    spread = lax.all_gather(tile, ("x", "h", "k"))
    images = (
        spread.reshape(16, 2, 2, 2, 10, 512)
        .transpose(1, 2, 3, 0, 4, 5)
        .reshape(2, 2, 2, cols, 512)
    )
    kernel2 = conv2_weight.transpose(0, 1, 2, 4, 3).reshape(27 * 32, 512)
    held, to_above, to_below = run(
        cache_conv,
        [((128, cols), F32), ((2, 80, 128), BF16), ((2, 80, 128), BF16)],
        (images, kernel2),
        16,
    )
    stats2, going_up, going_down = run(
        functools.partial(row_stats, peers=peers),
        [((peers, 1, 128), F32), ((10, 80, 128), BF16), ((10, 80, 128), BF16)],
        (gathered, to_above, to_below),
    )
    row_above = lax.ppermute(going_down, space, down)
    row_below = lax.ppermute(going_up, space, up)
    stats2 = lax.all_to_all(stats2, space, 0, 0, tiled=True)
    affine2, bias_here = run(
        up_columns,
        [((512, 2), F32), ((128, 1), F32)],
        (norm2_gain[None], norm2_bias[None], conv2_bias[None]),
    )
    lhs = run(up_weights, ((3 * 32, 3 * 512), BF16), (kernel2,))
    out = run(
        functools.partial(up_conv, sizes=sizes),
        ((16, cols // 16, 128), BF16),
        (
            stats2,
            gathered,
            row_above,
            row_below,
            affine2,
            lhs,
            held,
            bias_here,
        ),
        16,
    )
    out = lax.all_to_all(out, ("x", "h", "k"), 0, 0, tiled=True)
    out = out.reshape(16, 10, 2, 2, 32).transpose(2, 1, 3, 0, 4)
    return out.reshape(1, 2, 20, 512)


def solution(mesh):
    peers = mesh.shape["space"]
    n_l = 8 if peers % 8 == 0 else 2
    n_y = peers // n_l
    fine = Mesh(mesh.devices.reshape(n_y, n_l, 4, 2, 2), ("y", "l", "x", "h", "k"))
    space, chan = ("y", "l"), ("x", "h", "k")
    placed = (
        P(None, space, None, chan),
        P(None, space, None, chan),
        P(chan),
        P(chan),
        P(None, None, None, chan, None),
        P(chan),
        P(None, space, chan, None),
        P(),
        P(),
        P(None, None, None, None, chan),
        P(),
    )

    def body(*args):
        return on_device((n_y, n_l), *args)

    return jax.shard_map(
        body,
        mesh=fine,
        in_specs=placed,
        out_specs=P(None, space, chan, None),
        check_vma=False,
    )
```

```python
import functools

import jax
import jax.numpy as jnp
from jax import lax
from jax.experimental import pallas as pl
from jax.experimental.pallas import tpu as pltpu
from jax.sharding import Mesh
from jax.sharding import PartitionSpec as P


GS = 16
EPS = 1e-06
F32 = jnp.float32
BF16 = jnp.bfloat16
USE_KERNELS = True
FIRST_GRANT = 56


def run(fn, out_shapes, args, grant=8, late=()):
    if not USE_KERNELS:
        return fn(*[(lambda a=a: a) if i in late else a for i, a in enumerate(args)])
    n_a, single = len(args), isinstance(out_shapes, tuple)
    shapes = [out_shapes] if single else list(out_shapes)
    n_o = len(shapes)

    def body(*refs):
        held = refs[n_a + n_o :]
        ins = [None if i in late else r[...] for i, r in enumerate(refs[:n_a])]
        for spot, i in enumerate(late):
            copy = pltpu.make_async_copy(refs[i], held[2 * spot], held[2 * spot + 1])
            copy.start()

            def ready(copy=copy, buffer=held[2 * spot]):
                copy.wait()
                return buffer[...]

            ins[i] = ready
        outs = fn(*ins)
        outs = [outs] if single else outs
        for ref, value in zip(refs[n_a : n_a + n_o], outs):
            ref[...] = value

    vmem = pl.BlockSpec(memory_space=pltpu.VMEM)
    far = pl.BlockSpec(memory_space=pltpu.HBM)
    scratch = []
    for i in late:
        scratch += [pltpu.VMEM(args[i].shape, args[i].dtype), pltpu.SemaphoreType.DMA]
    res = pl.pallas_call(
        body,
        out_shape=[jax.ShapeDtypeStruct(s, d) for s, d in shapes],
        in_specs=[far if i in late else vmem for i in range(n_a)],
        out_specs=[vmem] * n_o,
        scratch_shapes=scratch,
        compiler_params=pltpu.CompilerParams(vmem_limit_bytes=grant << 20),
    )(*args)
    return res[0] if single else res


def to_row(col):
    n = col.shape[0]
    eye = lax.broadcasted_iota(jnp.int32, (n, n), 0) == lax.broadcasted_iota(jnp.int32, (n, n), 1)
    return jnp.sum(jnp.where(eye, col, 0.0), axis=0, keepdims=True)


def to_col(row, repeat):
    n = row.shape[1]
    rows = lax.broadcasted_iota(jnp.int32, (n * repeat, n), 0)
    lanes = lax.broadcasted_iota(jnp.int32, (n * repeat, n), 1)
    pick = (rows >= lanes * repeat) & (rows < lanes * repeat + repeat)
    return jnp.sum(jnp.where(pick, row, 0.0), axis=1, keepdims=True)


def partial_stats(values, peers):
    rows, cols = values.shape
    groups = rows // GS
    x = values.astype(F32)
    mean = jnp.sum(jnp.sum(x, axis=1, keepdims=True).reshape(groups, GS, 1), axis=1) / (GS * cols)
    dev = x.reshape(groups, GS, cols) - mean[:, :, None]
    sq = jnp.sum(jnp.sum(dev * dev, axis=2, keepdims=True), axis=1)
    row = jnp.concatenate(
        [to_row(mean), to_row(sq), jnp.zeros((1, 128 - 2 * groups), F32)], axis=1
    )
    return jnp.broadcast_to(row[None], (peers, 1, 128))


def merge_stats(parts, groups, count):
    peers = parts.shape[0]
    means = parts[:, 0, :groups]
    sq = parts[:, 0, groups : 2 * groups]
    mean = jnp.sum(means, axis=0, keepdims=True) / peers
    gap = means - mean
    var = (jnp.sum(sq, axis=0, keepdims=True) + count * jnp.sum(gap * gap, axis=0, keepdims=True)) / (
        count * peers
    )
    return mean, lax.rsqrt(var + EPS)


def norm_silu(x, mean, scale, gain, bias):
    v = (x.astype(F32) - mean) * scale * gain + bias
    low = v < -80.0
    e = jnp.exp(jnp.where(low, v, -v))
    return jnp.where(low, v * e, v / (1.0 + jnp.where(low, 0.0, e)))


def wide_col(row):
    n = row.shape[1]
    return jnp.concatenate([to_col(row[:, i : i + 128], 1) for i in range(0, n, 128)], axis=0)


def pack(a):
    tail = jnp.concatenate([a[16 * i : 16 * i + 16, 128:] for i in range(4)], axis=1)
    return jnp.concatenate([a[:, :128], tail], axis=0)


def unpack(a):
    tail = jnp.concatenate([a[64:, 32 * i : 32 * i + 32] for i in range(4)], axis=0)
    return jnp.concatenate([a[:64], tail], axis=1)


def right(a):
    return jnp.concatenate([jnp.zeros((a.shape[0], 1), a.dtype), a[:, :-1]], axis=1)


def left(a):
    return jnp.concatenate([a[:, 1:], jnp.zeros((a.shape[0], 1), a.dtype)], axis=1)


def edges(sizes):
    n_y, n_l = sizes
    row = lax.axis_index("y") * n_l + lax.axis_index("l")
    return row > 0, row < n_y * n_l - 1


def first_pass(own, cache, gain, bias, late_bias, peers):
    cols = jnp.concatenate([to_col(v, 1) for v in (gain, bias, late_bias)], axis=1)
    return partial_stats(own, peers), jnp.concatenate([cache, own[None]], axis=0), cols


def mid_conv(parts, raw, above, below, affine, kernel, sizes):
    chans, cols = raw.shape[1:]
    groups = chans // GS
    mean, scale = merge_stats(parts, groups, GS * cols)
    mean, scale = to_col(mean, GS), to_col(scale, GS)
    gain, bias = affine[:, :1], affine[:, 1:2]
    has = edges(sizes)
    pieces = []
    for t in range(3):
        for dy, src in enumerate((above, raw, below)):
            x = src[t].astype(F32)
            if t == 2:
                x = norm_silu(x, mean, scale, gain, bias)
                if dy != 1:
                    x = jnp.where(has[0 if dy == 0 else 1], x, 0.0)
            pieces += [right(x).astype(BF16), x.astype(BF16), left(x).astype(BF16)]
    columns = jnp.concatenate(pieces, axis=0)
    out = jnp.dot(columns.T, kernel(), preferred_element_type=F32).T
    blocks = []
    for x in range(4):
        for k in range(2):
            both = [out[(x * 4 + h * 2 + k) * 32 :][:32] for h in range(2)]
            blocks.append(pack(jnp.concatenate(both, axis=0)))
    return jnp.stack(blocks)


def fold(parts, own, affine):
    total = unpack(jnp.sum(parts, axis=0))
    extra = own.astype(F32) + affine[:, 2:3]
    zero = jnp.zeros_like(extra)
    first = lax.axis_index("h") == 0
    return pack(
        total
        + jnp.concatenate([jnp.where(first, extra, zero), jnp.where(first, zero, extra)], axis=0)
    )


def merge(mine, other):
    merged = (mine + other).astype(BF16)
    return jnp.broadcast_to(merged[None], (8,) + merged.shape)


def rows_of(gathered):
    blocks = [unpack(gathered[i].astype(F32)) for i in range(8)]
    return jnp.concatenate(
        [
            blocks[x * 2 + k][h * 32 : (h + 1) * 32]
            for x in range(4)
            for h in range(2)
            for k in range(2)
        ],
        axis=0,
    )


def row_stats(gathered, to_above, to_below, peers):
    return (
        partial_stats(rows_of(gathered), peers),
        jnp.concatenate([gathered, to_above], axis=0),
        jnp.concatenate([gathered, to_below], axis=0),
    )


def halves(a):
    a = pack(a)
    high = a.astype(BF16)
    return jnp.stack([high, (a - high.astype(F32)).astype(BF16)])


def whole(blocks):
    return unpack(blocks[0].astype(F32) + blocks[1].astype(F32))


def taps(prod):
    return [[prod[(dy * 3 + dx) * 32 : (dy * 3 + dx + 1) * 32] for dx in range(3)] for dy in range(3)]


def cache_conv(images, kernel):
    per = 9 * 32
    sums = {}

    def add(key, value):
        sums[key] = sums[key] + value if key in sums else value

    for t in range(2):
        w = kernel[t * per : (t + 1) * per]
        for r in range(2):
            even, odd = (
                taps(
                    lax.dot_general(
                        w, images[t, r, p], (((1,), (1,)), ((), ())), preferred_element_type=F32
                    )
                )
                for p in range(2)
            )
            for dy in range(3):
                o = r + 1 - dy
                add((o, "m", 0), even[dy][1] + odd[dy][2])
                add((o, "r", 0), odd[dy][0])
                add((o, "m", 1), even[dy][0] + odd[dy][1])
                add((o, "l", 1), even[dy][2])

    def out(o):
        return jnp.concatenate(
            [
                sums[(o, "m", 0)] + right(sums[(o, "r", 0)]),
                sums[(o, "m", 1)] + left(sums[(o, "l", 1)]),
            ],
            axis=0,
        )

    return jnp.concatenate([out(0), out(1)], axis=0), halves(out(-1)), halves(out(2))


def up_columns(gain, bias, out_bias):
    chan = lax.axis_index("x") * 4 + lax.axis_index("h") * 2 + lax.axis_index("k")
    rows = lax.broadcasted_iota(jnp.int32, (32, out_bias.shape[1]), 0)
    lanes = lax.broadcasted_iota(jnp.int32, (32, out_bias.shape[1]), 1)
    picked = jnp.sum(jnp.where(lanes == rows + chan * 32, out_bias, 0.0), axis=1, keepdims=True)
    return jnp.concatenate([wide_col(gain), wide_col(bias)], axis=1), jnp.concatenate(
        [picked] * 4, axis=0
    )


def up_weights(kernel):
    return jnp.concatenate(
        [kernel[(18 + dy * 3) * 32 : (21 + dy * 3) * 32] for dy in range(3)], axis=1
    )


def up_conv(parts, row, above, below, affine, lhs, held, out_bias, sizes):
    from_above, from_below = whole(above[8:]), whole(below[8:])
    row, above, below = rows_of(row), rows_of(above[:8]), rows_of(below[:8])
    chans, cols = row.shape
    groups = chans // GS
    mean, scale = merge_stats(parts, groups, GS * cols)
    mean, scale = to_col(mean, GS), to_col(scale, GS)
    gain, bias = affine[:, :1], affine[:, 1:2]
    has = edges(sizes)

    def image(x, keep=None):
        v = norm_silu(x, mean, scale, gain, bias)
        if keep is not None:
            v = jnp.where(keep, v, 0.0)
        return v.astype(BF16)

    here = image(row)
    outs = []
    for images in ((image(above, has[0]), here, here), (here, here, image(below, has[1]))):
        prod = jnp.dot(lhs, jnp.concatenate(images, axis=0), preferred_element_type=F32)
        cut = [prod[dx * 32 : (dx + 1) * 32] for dx in range(3)]
        outs += [right(cut[0]) + cut[1] + cut[2], cut[0] + cut[1] + left(cut[2])]
    total = jnp.concatenate(outs, axis=0) + held
    total = total + jnp.concatenate([from_above, from_below], axis=0)
    total = (total + out_bias).T
    part = cols // 16
    return jnp.stack([total[c * part : (c + 1) * part] for c in range(16)]).astype(BF16)


def on_device(
    sizes,
    latent,
    cache_mid,
    norm1_gain,
    norm1_bias,
    conv1_weight,
    conv1_bias,
    cache_up,
    norm2_gain,
    norm2_bias,
    conv2_weight,
    conv2_bias,
):
    n_y, n_l = sizes
    peers = n_y * n_l
    cols, chans = latent.shape[2], latent.shape[3]
    sizes = (n_y, n_l)
    hi = lax.axis_index("h")
    space = ("y", "l")
    own = latent[0, 0].T
    stats, raw, affine = run(
        functools.partial(first_pass, peers=peers),
        [((peers, 1, 128), F32), ((3, chans, cols), BF16), ((chans, 3), F32)],
        (own, cache_mid[:, 0].transpose(0, 2, 1), norm1_gain[None], norm1_bias[None], conv1_bias[None]),
        FIRST_GRANT,
    )
    stats = lax.all_to_all(stats, space, 0, 0, tiled=True)
    down = [(i, i + 1) for i in range(peers - 1)]
    up = [(i + 1, i) for i in range(peers - 1)]
    above = lax.ppermute(raw, space, down)
    below = lax.ppermute(raw, space, up)
    partial = run(
        functools.partial(mid_conv, sizes=sizes),
        ((8, 80, 128), F32),
        (stats, raw, above, below, affine, conv1_weight.reshape(27 * chans, 512)),
        FIRST_GRANT,
        late=(5,),
    )
    partial = lax.all_to_all(partial, ("x", "k"), 0, 0, tiled=True)
    mine = run(fold, ((80, 128), F32), (partial, own, affine))
    other = lax.ppermute(mine, "h", [(0, 1), (1, 0)])
    gathered = run(merge, ((8, 80, 128), BF16), (mine, other))
    gathered = lax.all_to_all(gathered, ("x", "k"), 0, 0, tiled=True)
    tile = cache_up.reshape(2, 2, 10, 2, 512).transpose(0, 1, 3, 2, 4)
    swapped = lax.ppermute(tile, "h", [(0, 1), (1, 0)])
    pair = jnp.where(hi == 0, jnp.stack([tile, swapped]), jnp.stack([swapped, tile]))
    copies = jnp.broadcast_to(pair[None], (8,) + pair.shape)
    spread = lax.all_to_all(copies, ("x", "k"), 0, 0, tiled=True)
    images = (
        spread.reshape(4, 2, 2, 2, 2, 2, 10, 512)
        .transpose(3, 4, 5, 0, 2, 1, 6, 7)
        .reshape(2, 2, 2, cols, 512)
    )
    kernel2 = conv2_weight.transpose(0, 1, 2, 4, 3).reshape(27 * 32, 512)
    held, to_above, to_below = run(
        cache_conv,
        [((128, cols), F32), ((2, 80, 128), BF16), ((2, 80, 128), BF16)],
        (images, kernel2),
        16,
    )
    stats2, going_up, going_down = run(
        functools.partial(row_stats, peers=peers),
        [((peers, 1, 128), F32), ((10, 80, 128), BF16), ((10, 80, 128), BF16)],
        (gathered, to_above, to_below),
    )
    row_above = lax.ppermute(going_down, space, down)
    row_below = lax.ppermute(going_up, space, up)
    stats2 = lax.all_to_all(stats2, space, 0, 0, tiled=True)
    affine2, bias_here = run(
        up_columns,
        [((512, 2), F32), ((128, 1), F32)],
        (norm2_gain[None], norm2_bias[None], conv2_bias[None]),
    )
    lhs = run(up_weights, ((3 * 32, 3 * 512), BF16), (kernel2,))
    out = run(
        functools.partial(up_conv, sizes=sizes),
        ((16, cols // 16, 128), BF16),
        (
            stats2,
            gathered,
            row_above,
            row_below,
            affine2,
            lhs,
            held,
            bias_here,
        ),
        16,
    )
    out = lax.all_to_all(out, ("x", "h", "k"), 0, 0, tiled=True)
    out = out.reshape(16, 10, 2, 2, 32).transpose(2, 1, 3, 0, 4)
    return out.reshape(1, 2, 20, 512)


def solution(mesh):
    peers = mesh.shape["space"]
    n_l = 8 if peers % 8 == 0 else 2
    n_y = peers // n_l
    fine = Mesh(mesh.devices.reshape(n_y, n_l, 4, 2, 2), ("y", "l", "x", "h", "k"))
    space, chan = ("y", "l"), ("x", "h", "k")
    placed = (
        P(None, space, None, chan),
        P(None, space, None, chan),
        P(chan),
        P(chan),
        P(None, None, None, chan, None),
        P(chan),
        P(None, space, chan, None),
        P(),
        P(),
        P(None, None, None, None, chan),
        P(),
    )

    def body(*args):
        return on_device((n_y, n_l), *args)

    return jax.shard_map(
        body,
        mesh=fine,
        in_specs=placed,
        out_specs=P(None, space, chan, None),
        check_vma=False,
    )
```

```python
import functools

import jax
import jax.numpy as jnp
from jax import lax
from jax.experimental import pallas as pl
from jax.experimental.pallas import tpu as pltpu
from jax.sharding import Mesh
from jax.sharding import PartitionSpec as P


GS = 16
EPS = 1e-06
F32 = jnp.float32
BF16 = jnp.bfloat16
USE_KERNELS = True
FIRST_GRANT = 56


def run(fn, out_shapes, args, grant=8):
    if not USE_KERNELS:
        return fn(*args)
    n_a, single = len(args), isinstance(out_shapes, tuple)
    shapes = [out_shapes] if single else list(out_shapes)

    def body(*refs):
        outs = fn(*[r[...] for r in refs[:n_a]])
        outs = [outs] if single else outs
        for ref, value in zip(refs[n_a:], outs):
            ref[...] = value

    vmem = pl.BlockSpec(memory_space=pltpu.VMEM)
    res = pl.pallas_call(
        body,
        out_shape=[jax.ShapeDtypeStruct(s, d) for s, d in shapes],
        in_specs=[vmem] * n_a,
        out_specs=[vmem] * len(shapes),
        compiler_params=pltpu.CompilerParams(vmem_limit_bytes=grant << 20),
    )(*args)
    return res[0] if single else res


def preload(array):
    if not USE_KERNELS:
        return array
    return pl.pallas_call(
        lambda source, target: pltpu.sync_copy(source, target),
        out_shape=jax.ShapeDtypeStruct(array.shape, array.dtype),
        in_specs=[pl.BlockSpec(memory_space=pltpu.HBM)],
        out_specs=pl.BlockSpec(memory_space=pltpu.VMEM),
        compiler_params=pltpu.CompilerParams(vmem_limit_bytes=4 << 20),
    )(array)


def to_row(col):
    n = col.shape[0]
    eye = lax.broadcasted_iota(jnp.int32, (n, n), 0) == lax.broadcasted_iota(jnp.int32, (n, n), 1)
    return jnp.sum(jnp.where(eye, col, 0.0), axis=0, keepdims=True)


def to_col(row, repeat):
    n = row.shape[1]
    rows = lax.broadcasted_iota(jnp.int32, (n * repeat, n), 0)
    lanes = lax.broadcasted_iota(jnp.int32, (n * repeat, n), 1)
    pick = (rows >= lanes * repeat) & (rows < lanes * repeat + repeat)
    return jnp.sum(jnp.where(pick, row, 0.0), axis=1, keepdims=True)


def partial_stats(values, peers):
    rows, cols = values.shape
    groups = rows // GS
    x = values.astype(F32)
    mean = jnp.sum(jnp.sum(x, axis=1, keepdims=True).reshape(groups, GS, 1), axis=1) / (GS * cols)
    dev = x.reshape(groups, GS, cols) - mean[:, :, None]
    sq = jnp.sum(jnp.sum(dev * dev, axis=2, keepdims=True), axis=1)
    row = jnp.concatenate(
        [to_row(mean), to_row(sq), jnp.zeros((1, 128 - 2 * groups), F32)], axis=1
    )
    return jnp.broadcast_to(row[None], (peers, 1, 128))


def merge_stats(parts, groups, count):
    peers = parts.shape[0]
    means = parts[:, 0, :groups]
    sq = parts[:, 0, groups : 2 * groups]
    mean = jnp.sum(means, axis=0, keepdims=True) / peers
    gap = means - mean
    var = (jnp.sum(sq, axis=0, keepdims=True) + count * jnp.sum(gap * gap, axis=0, keepdims=True)) / (
        count * peers
    )
    return mean, lax.rsqrt(var + EPS)


def norm_silu(x, mean, scale, gain, bias):
    v = (x.astype(F32) - mean) * scale * gain + bias
    low = v < -80.0
    e = jnp.exp(jnp.where(low, v, -v))
    return jnp.where(low, v * e, v / (1.0 + jnp.where(low, 0.0, e)))


def wide_col(row):
    n = row.shape[1]
    return jnp.concatenate([to_col(row[:, i : i + 128], 1) for i in range(0, n, 128)], axis=0)


def pack(a):
    tail = jnp.concatenate([a[16 * i : 16 * i + 16, 128:] for i in range(4)], axis=1)
    return jnp.concatenate([a[:, :128], tail], axis=0)


def unpack(a):
    tail = jnp.concatenate([a[64:, 32 * i : 32 * i + 32] for i in range(4)], axis=0)
    return jnp.concatenate([a[:64], tail], axis=1)


def right(a):
    return jnp.concatenate([jnp.zeros((a.shape[0], 1), a.dtype), a[:, :-1]], axis=1)


def left(a):
    return jnp.concatenate([a[:, 1:], jnp.zeros((a.shape[0], 1), a.dtype)], axis=1)


def edges(sizes):
    n_y, n_l = sizes
    row = lax.axis_index("y") * n_l + lax.axis_index("l")
    return row > 0, row < n_y * n_l - 1


def first_pass(own, cache, gain, bias, late_bias, peers):
    cols = jnp.concatenate([to_col(v, 1) for v in (gain, bias, late_bias)], axis=1)
    return partial_stats(own, peers), jnp.concatenate([cache, own[None]], axis=0), cols


def mid_conv(parts, raw, above, below, affine, kernel, sizes):
    chans, cols = raw.shape[1:]
    groups = chans // GS
    mean, scale = merge_stats(parts, groups, GS * cols)
    mean, scale = to_col(mean, GS), to_col(scale, GS)
    gain, bias = affine[:, :1], affine[:, 1:2]
    has = edges(sizes)
    pieces = []
    for t in range(3):
        for dy, src in enumerate((above, raw, below)):
            x = src[t].astype(F32)
            if t == 2:
                x = norm_silu(x, mean, scale, gain, bias)
                if dy != 1:
                    x = jnp.where(has[0 if dy == 0 else 1], x, 0.0)
            pieces += [right(x).astype(BF16), x.astype(BF16), left(x).astype(BF16)]
    columns = jnp.concatenate(pieces, axis=0)
    out = jnp.dot(columns.T, kernel, preferred_element_type=F32).T
    blocks = []
    for x in range(4):
        for k in range(2):
            both = [out[(x * 4 + h * 2 + k) * 32 :][:32] for h in range(2)]
            blocks.append(pack(jnp.concatenate(both, axis=0)))
    return jnp.stack(blocks)


def fold(parts, own, affine):
    total = unpack(jnp.sum(parts, axis=0))
    extra = own.astype(F32) + affine[:, 2:3]
    zero = jnp.zeros_like(extra)
    first = lax.axis_index("h") == 0
    return pack(
        total
        + jnp.concatenate([jnp.where(first, extra, zero), jnp.where(first, zero, extra)], axis=0)
    )


def merge(mine, other):
    merged = (mine + other).astype(BF16)
    return jnp.broadcast_to(merged[None], (8,) + merged.shape)


def rows_of(gathered):
    blocks = [unpack(gathered[i].astype(F32)) for i in range(8)]
    return jnp.concatenate(
        [
            blocks[x * 2 + k][h * 32 : (h + 1) * 32]
            for x in range(4)
            for h in range(2)
            for k in range(2)
        ],
        axis=0,
    )


def row_stats(gathered, to_above, to_below, peers):
    return (
        partial_stats(rows_of(gathered), peers),
        jnp.concatenate([gathered, to_above], axis=0),
        jnp.concatenate([gathered, to_below], axis=0),
    )


def halves(a):
    a = pack(a)
    high = a.astype(BF16)
    return jnp.stack([high, (a - high.astype(F32)).astype(BF16)])


def whole(blocks):
    return unpack(blocks[0].astype(F32) + blocks[1].astype(F32))


def taps(prod):
    return [[prod[(dy * 3 + dx) * 32 : (dy * 3 + dx + 1) * 32] for dx in range(3)] for dy in range(3)]


def cache_conv(images, kernel):
    per = 9 * 32
    sums = {}

    def add(key, value):
        sums[key] = sums[key] + value if key in sums else value

    for t in range(2):
        w = kernel[t * per : (t + 1) * per]
        for r in range(2):
            even, odd = (
                taps(
                    lax.dot_general(
                        w, images[t, r, p], (((1,), (1,)), ((), ())), preferred_element_type=F32
                    )
                )
                for p in range(2)
            )
            for dy in range(3):
                o = r + 1 - dy
                add((o, "m", 0), even[dy][1] + odd[dy][2])
                add((o, "r", 0), odd[dy][0])
                add((o, "m", 1), even[dy][0] + odd[dy][1])
                add((o, "l", 1), even[dy][2])

    def out(o):
        return jnp.concatenate(
            [
                sums[(o, "m", 0)] + right(sums[(o, "r", 0)]),
                sums[(o, "m", 1)] + left(sums[(o, "l", 1)]),
            ],
            axis=0,
        )

    return jnp.concatenate([out(0), out(1)], axis=0), halves(out(-1)), halves(out(2))


def up_columns(gain, bias, out_bias):
    chan = lax.axis_index("x") * 4 + lax.axis_index("h") * 2 + lax.axis_index("k")
    rows = lax.broadcasted_iota(jnp.int32, (32, out_bias.shape[1]), 0)
    lanes = lax.broadcasted_iota(jnp.int32, (32, out_bias.shape[1]), 1)
    picked = jnp.sum(jnp.where(lanes == rows + chan * 32, out_bias, 0.0), axis=1, keepdims=True)
    return jnp.concatenate([wide_col(gain), wide_col(bias)], axis=1), jnp.concatenate(
        [picked] * 4, axis=0
    )


def up_weights(kernel):
    return jnp.concatenate(
        [kernel[(18 + dy * 3) * 32 : (21 + dy * 3) * 32] for dy in range(3)], axis=1
    )


def up_conv(parts, row, above, below, affine, lhs, held, out_bias, sizes):
    from_above, from_below = whole(above[8:]), whole(below[8:])
    row, above, below = rows_of(row), rows_of(above[:8]), rows_of(below[:8])
    chans, cols = row.shape
    groups = chans // GS
    mean, scale = merge_stats(parts, groups, GS * cols)
    mean, scale = to_col(mean, GS), to_col(scale, GS)
    gain, bias = affine[:, :1], affine[:, 1:2]
    has = edges(sizes)

    def image(x, keep=None):
        v = norm_silu(x, mean, scale, gain, bias)
        if keep is not None:
            v = jnp.where(keep, v, 0.0)
        return v.astype(BF16)

    here = image(row)
    outs = []
    for images in ((image(above, has[0]), here, here), (here, here, image(below, has[1]))):
        prod = jnp.dot(lhs, jnp.concatenate(images, axis=0), preferred_element_type=F32)
        cut = [prod[dx * 32 : (dx + 1) * 32] for dx in range(3)]
        outs += [right(cut[0]) + cut[1] + cut[2], cut[0] + cut[1] + left(cut[2])]
    total = jnp.concatenate(outs, axis=0) + held
    total = total + jnp.concatenate([from_above, from_below], axis=0)
    total = (total + out_bias).T
    part = cols // 16
    return jnp.stack([total[c * part : (c + 1) * part] for c in range(16)]).astype(BF16)


def on_device(
    sizes,
    latent,
    cache_mid,
    norm1_gain,
    norm1_bias,
    conv1_weight,
    conv1_bias,
    cache_up,
    norm2_gain,
    norm2_bias,
    conv2_weight,
    conv2_bias,
):
    n_y, n_l = sizes
    peers = n_y * n_l
    cols, chans = latent.shape[2], latent.shape[3]
    sizes = (n_y, n_l)
    hi = lax.axis_index("h")
    space = ("y", "l")
    own = latent[0, 0].T
    stats, raw, affine = run(
        functools.partial(first_pass, peers=peers),
        [((peers, 1, 128), F32), ((3, chans, cols), BF16), ((chans, 3), F32)],
        (own, cache_mid[:, 0].transpose(0, 2, 1), norm1_gain[None], norm1_bias[None], conv1_bias[None]),
        FIRST_GRANT,
    )
    stats = lax.all_to_all(stats, space, 0, 0, tiled=True)
    down = [(i, i + 1) for i in range(peers - 1)]
    up = [(i + 1, i) for i in range(peers - 1)]
    above = lax.ppermute(raw, space, down)
    below = lax.ppermute(raw, space, up)
    partial = run(
        functools.partial(mid_conv, sizes=sizes),
        ((8, 80, 128), F32),
        (stats, raw, above, below, affine, preload(conv1_weight.reshape(27 * chans, 512))),
    )
    partial = lax.all_to_all(partial, ("x", "k"), 0, 0, tiled=True)
    mine = run(fold, ((80, 128), F32), (partial, own, affine))
    other = lax.ppermute(mine, "h", [(0, 1), (1, 0)])
    gathered = run(merge, ((8, 80, 128), BF16), (mine, other))
    gathered = lax.all_to_all(gathered, ("x", "k"), 0, 0, tiled=True)
    tile = cache_up.reshape(2, 2, 10, 2, 512).transpose(0, 1, 3, 2, 4)
    swapped = lax.ppermute(tile, "h", [(0, 1), (1, 0)])
    pair = jnp.where(hi == 0, jnp.stack([tile, swapped]), jnp.stack([swapped, tile]))
    copies = jnp.broadcast_to(pair[None], (8,) + pair.shape)
    spread = lax.all_to_all(copies, ("x", "k"), 0, 0, tiled=True)
    images = (
        spread.reshape(4, 2, 2, 2, 2, 2, 10, 512)
        .transpose(3, 4, 5, 0, 2, 1, 6, 7)
        .reshape(2, 2, 2, cols, 512)
    )
    kernel2 = conv2_weight.transpose(0, 1, 2, 4, 3).reshape(27 * 32, 512)
    held, to_above, to_below = run(
        cache_conv,
        [((128, cols), F32), ((2, 80, 128), BF16), ((2, 80, 128), BF16)],
        (images, kernel2),
        16,
    )
    stats2, going_up, going_down = run(
        functools.partial(row_stats, peers=peers),
        [((peers, 1, 128), F32), ((10, 80, 128), BF16), ((10, 80, 128), BF16)],
        (gathered, to_above, to_below),
    )
    row_above = lax.ppermute(going_down, space, down)
    row_below = lax.ppermute(going_up, space, up)
    stats2 = lax.all_to_all(stats2, space, 0, 0, tiled=True)
    affine2, bias_here = run(
        up_columns,
        [((512, 2), F32), ((128, 1), F32)],
        (norm2_gain[None], norm2_bias[None], conv2_bias[None]),
    )
    lhs = run(up_weights, ((3 * 32, 3 * 512), BF16), (kernel2,))
    out = run(
        functools.partial(up_conv, sizes=sizes),
        ((16, cols // 16, 128), BF16),
        (
            stats2,
            gathered,
            row_above,
            row_below,
            affine2,
            lhs,
            held,
            bias_here,
        ),
        16,
    )
    out = lax.all_to_all(out, ("x", "h", "k"), 0, 0, tiled=True)
    out = out.reshape(16, 10, 2, 2, 32).transpose(2, 1, 3, 0, 4)
    return out.reshape(1, 2, 20, 512)


def solution(mesh):
    peers = mesh.shape["space"]
    n_l = 8 if peers % 8 == 0 else 2
    n_y = peers // n_l
    fine = Mesh(mesh.devices.reshape(n_y, n_l, 4, 2, 2), ("y", "l", "x", "h", "k"))
    space, chan = ("y", "l"), ("x", "h", "k")
    placed = (
        P(None, space, None, chan),
        P(None, space, None, chan),
        P(chan),
        P(chan),
        P(None, None, None, chan, None),
        P(chan),
        P(None, space, chan, None),
        P(),
        P(),
        P(None, None, None, None, chan),
        P(),
    )

    def body(*args):
        return on_device((n_y, n_l), *args)

    return jax.shard_map(
        body,
        mesh=fine,
        in_specs=placed,
        out_specs=P(None, space, chan, None),
        check_vma=False,
    )
```

```python
import functools

import jax
import jax.numpy as jnp
from jax import lax
from jax.experimental import pallas as pl
from jax.experimental.pallas import tpu as pltpu
from jax.sharding import Mesh
from jax.sharding import PartitionSpec as P


GS = 16
EPS = 1e-06
F32 = jnp.float32
BF16 = jnp.bfloat16
USE_KERNELS = True
FIRST_GRANT = 56


def run(fn, out_shapes, args, grant=8):
    if not USE_KERNELS:
        return fn(*args)
    n_a, single = len(args), isinstance(out_shapes, tuple)
    shapes = [out_shapes] if single else list(out_shapes)

    def body(*refs):
        outs = fn(*[r[...] for r in refs[:n_a]])
        outs = [outs] if single else outs
        for ref, value in zip(refs[n_a:], outs):
            ref[...] = value

    vmem = pl.BlockSpec(memory_space=pltpu.VMEM)
    res = pl.pallas_call(
        body,
        out_shape=[jax.ShapeDtypeStruct(s, d) for s, d in shapes],
        in_specs=[vmem] * n_a,
        out_specs=[vmem] * len(shapes),
        compiler_params=pltpu.CompilerParams(vmem_limit_bytes=grant << 20),
    )(*args)
    return res[0] if single else res


def preload(array):
    if not USE_KERNELS:
        return array
    return pl.pallas_call(
        lambda source, target: pltpu.sync_copy(source, target),
        out_shape=jax.ShapeDtypeStruct(array.shape, array.dtype),
        in_specs=[pl.BlockSpec(memory_space=pltpu.HBM)],
        out_specs=pl.BlockSpec(memory_space=pltpu.VMEM),
        compiler_params=pltpu.CompilerParams(vmem_limit_bytes=4 << 20),
    )(array)


def to_row(col):
    n = col.shape[0]
    eye = lax.broadcasted_iota(jnp.int32, (n, n), 0) == lax.broadcasted_iota(jnp.int32, (n, n), 1)
    return jnp.sum(jnp.where(eye, col, 0.0), axis=0, keepdims=True)


def to_col(row, repeat):
    n = row.shape[1]
    rows = lax.broadcasted_iota(jnp.int32, (n * repeat, n), 0)
    lanes = lax.broadcasted_iota(jnp.int32, (n * repeat, n), 1)
    pick = (rows >= lanes * repeat) & (rows < lanes * repeat + repeat)
    return jnp.sum(jnp.where(pick, row, 0.0), axis=1, keepdims=True)


def partial_stats(values, peers):
    rows, cols = values.shape
    groups = rows // GS
    x = values.astype(F32)
    mean = jnp.sum(jnp.sum(x, axis=1, keepdims=True).reshape(groups, GS, 1), axis=1) / (GS * cols)
    dev = x.reshape(groups, GS, cols) - mean[:, :, None]
    sq = jnp.sum(jnp.sum(dev * dev, axis=2, keepdims=True), axis=1)
    row = jnp.concatenate(
        [to_row(mean), to_row(sq), jnp.zeros((1, 128 - 2 * groups), F32)], axis=1
    )
    return jnp.broadcast_to(row[None], (peers, 1, 128))


def merge_stats(parts, groups, count):
    peers = parts.shape[0]
    means = parts[:, 0, :groups]
    sq = parts[:, 0, groups : 2 * groups]
    mean = jnp.sum(means, axis=0, keepdims=True) / peers
    gap = means - mean
    var = (jnp.sum(sq, axis=0, keepdims=True) + count * jnp.sum(gap * gap, axis=0, keepdims=True)) / (
        count * peers
    )
    return mean, lax.rsqrt(var + EPS)


def norm_silu(x, mean, scale, gain, bias):
    v = (x.astype(F32) - mean) * scale * gain + bias
    low = v < -80.0
    e = jnp.exp(jnp.where(low, v, -v))
    return jnp.where(low, v * e, v / (1.0 + jnp.where(low, 0.0, e)))


def wide_col(row):
    n = row.shape[1]
    return jnp.concatenate([to_col(row[:, i : i + 128], 1) for i in range(0, n, 128)], axis=0)


def pack(a):
    tail = jnp.concatenate([a[16 * i : 16 * i + 16, 128:] for i in range(4)], axis=1)
    return jnp.concatenate([a[:, :128], tail], axis=0)


def unpack(a):
    tail = jnp.concatenate([a[64:, 32 * i : 32 * i + 32] for i in range(4)], axis=0)
    return jnp.concatenate([a[:64], tail], axis=1)


def right(a):
    return jnp.concatenate([jnp.zeros((a.shape[0], 1), a.dtype), a[:, :-1]], axis=1)


def left(a):
    return jnp.concatenate([a[:, 1:], jnp.zeros((a.shape[0], 1), a.dtype)], axis=1)


def edges(sizes):
    n_y, n_l = sizes
    row = lax.axis_index("y") * n_l + lax.axis_index("l")
    return row > 0, row < n_y * n_l - 1


def first_pass(own, cache, gain, bias, late_bias, peers):
    cols = jnp.concatenate([to_col(v, 1) for v in (gain, bias, late_bias)], axis=1)
    return partial_stats(own, peers), jnp.concatenate([cache, own[None]], axis=0), cols


def mid_conv(parts, raw, above, below, affine, kernel, sizes):
    chans, cols = raw.shape[1:]
    groups = chans // GS
    mean, scale = merge_stats(parts, groups, GS * cols)
    mean, scale = to_col(mean, GS), to_col(scale, GS)
    gain, bias = affine[:, :1], affine[:, 1:2]
    has = edges(sizes)
    pieces = []
    for t in range(3):
        for dy, src in enumerate((above, raw, below)):
            x = src[t].astype(F32)
            if t == 2:
                x = norm_silu(x, mean, scale, gain, bias)
                if dy != 1:
                    x = jnp.where(has[0 if dy == 0 else 1], x, 0.0)
            pieces += [right(x).astype(BF16), x.astype(BF16), left(x).astype(BF16)]
    columns = jnp.concatenate(pieces, axis=0)
    out = jnp.dot(columns.T, kernel, preferred_element_type=F32).T
    blocks = []
    for x in range(4):
        for k in range(2):
            both = [out[(x * 4 + h * 2 + k) * 32 :][:32] for h in range(2)]
            blocks.append(pack(jnp.concatenate(both, axis=0)))
    return jnp.stack(blocks)


def fold(parts, own, affine):
    total = unpack(jnp.sum(parts, axis=0))
    extra = own.astype(F32) + affine[:, 2:3]
    zero = jnp.zeros_like(extra)
    first = lax.axis_index("h") == 0
    return pack(
        total
        + jnp.concatenate([jnp.where(first, extra, zero), jnp.where(first, zero, extra)], axis=0)
    )


def merge(mine, other):
    merged = (mine + other).astype(BF16)
    return jnp.broadcast_to(merged[None], (8,) + merged.shape)


def rows_of(gathered):
    blocks = [unpack(gathered[i].astype(F32)) for i in range(8)]
    return jnp.concatenate(
        [
            blocks[x * 2 + k][h * 32 : (h + 1) * 32]
            for x in range(4)
            for h in range(2)
            for k in range(2)
        ],
        axis=0,
    )


def row_stats(gathered, peers):
    return partial_stats(rows_of(gathered), peers)


def product(w, image):
    return lax.dot_general(w, image, (((1,), (1,)), ((), ())), preferred_element_type=F32)


def phases(even, odd):
    first = even[32:64] + odd[64:] + right(odd[:32])
    second = even[:32] + odd[32:64] + left(even[64:])
    return jnp.concatenate([first, second], axis=0)


def cache_conv(first, second, kernel):
    outs = []
    for o in range(2):
        sums = []
        for p in range(2):
            total = None
            for t in range(2):
                for r in range(2):
                    row = (t * 3 + r - o + 1) * 96
                    value = product(kernel[row : row + 96], (first, second)[r][t, p])
                    total = value if total is None else total + value
            sums.append(total)
        outs.append(phases(*sums))
    return jnp.concatenate(outs, axis=0)


def edge_conv(above, below, kernel):
    outs = []
    for image, dy in ((above, 0), (below, 2)):
        sums = [
            product(kernel[dy * 96 : dy * 96 + 96], image[0, p])
            + product(kernel[(3 + dy) * 96 : (4 + dy) * 96], image[1, p])
            for p in range(2)
        ]
        outs.append(phases(*sums))
    return jnp.concatenate(outs, axis=0)


def up_columns(gain, bias, out_bias):
    chan = lax.axis_index("x") * 4 + lax.axis_index("h") * 2 + lax.axis_index("k")
    rows = lax.broadcasted_iota(jnp.int32, (32, out_bias.shape[1]), 0)
    lanes = lax.broadcasted_iota(jnp.int32, (32, out_bias.shape[1]), 1)
    picked = jnp.sum(jnp.where(lanes == rows + chan * 32, out_bias, 0.0), axis=1, keepdims=True)
    return jnp.concatenate([wide_col(gain), wide_col(bias)], axis=1), jnp.concatenate(
        [picked] * 4, axis=0
    )


def up_weights(kernel):
    return jnp.concatenate(
        [kernel[(18 + dy * 3) * 32 : (21 + dy * 3) * 32] for dy in range(3)], axis=1
    )


def up_conv(parts, row, above, below, affine, lhs, held, out_bias, old_above, old_below, kernel, sizes):
    row, above, below = rows_of(row), rows_of(above), rows_of(below)
    chans, cols = row.shape
    groups = chans // GS
    mean, scale = merge_stats(parts, groups, GS * cols)
    mean, scale = to_col(mean, GS), to_col(scale, GS)
    gain, bias = affine[:, :1], affine[:, 1:2]
    has = edges(sizes)

    def image(x, keep=None):
        v = norm_silu(x, mean, scale, gain, bias)
        if keep is not None:
            v = jnp.where(keep, v, 0.0)
        return v.astype(BF16)

    here = image(row)
    outs = []
    for images in ((image(above, has[0]), here, here), (here, here, image(below, has[1]))):
        prod = jnp.dot(lhs, jnp.concatenate(images, axis=0), preferred_element_type=F32)
        cut = [prod[dx * 32 : (dx + 1) * 32] for dx in range(3)]
        outs += [right(cut[0]) + cut[1] + cut[2], cut[0] + cut[1] + left(cut[2])]
    total = jnp.concatenate(outs, axis=0) + held
    total = total + edge_conv(old_above, old_below, kernel)
    total = (total + out_bias).T
    part = cols // 16
    return jnp.stack([total[c * part : (c + 1) * part] for c in range(16)]).astype(BF16)


def on_device(
    sizes,
    latent,
    cache_mid,
    norm1_gain,
    norm1_bias,
    conv1_weight,
    conv1_bias,
    cache_up,
    norm2_gain,
    norm2_bias,
    conv2_weight,
    conv2_bias,
):
    n_y, n_l = sizes
    peers = n_y * n_l
    cols, chans = latent.shape[2], latent.shape[3]
    sizes = (n_y, n_l)
    hi = lax.axis_index("h")
    space = ("y", "l")
    own = latent[0, 0].T
    stats, raw, affine = run(
        functools.partial(first_pass, peers=peers),
        [((peers, 1, 128), F32), ((3, chans, cols), BF16), ((chans, 3), F32)],
        (own, cache_mid[:, 0].transpose(0, 2, 1), norm1_gain[None], norm1_bias[None], conv1_bias[None]),
        FIRST_GRANT,
    )
    stats = lax.all_to_all(stats, space, 0, 0, tiled=True)
    down = [(i, i + 1) for i in range(peers - 1)]
    up = [(i + 1, i) for i in range(peers - 1)]
    above = lax.ppermute(raw, space, down)
    below = lax.ppermute(raw, space, up)
    partial = run(
        functools.partial(mid_conv, sizes=sizes),
        ((8, 80, 128), F32),
        (stats, raw, above, below, affine, preload(conv1_weight.reshape(27 * chans, 512))),
    )
    partial = lax.all_to_all(partial, ("x", "k"), 0, 0, tiled=True)
    mine = run(fold, ((80, 128), F32), (partial, own, affine))
    other = lax.ppermute(mine, "h", [(0, 1), (1, 0)])
    gathered = run(merge, ((8, 80, 128), BF16), (mine, other))
    gathered = lax.all_to_all(gathered, ("x", "k"), 0, 0, tiled=True)
    tile = cache_up.reshape(2, 2, 10, 2, 512).transpose(0, 1, 3, 2, 4)
    swapped = lax.ppermute(tile, "h", [(0, 1), (1, 0)])
    pair = jnp.where(hi == 0, jnp.stack([tile, swapped]), jnp.stack([swapped, tile]))
    copies = jnp.broadcast_to(pair[None], (8,) + pair.shape)
    spread = lax.all_to_all(copies, ("x", "k"), 0, 0, tiled=True)
    spread = spread.reshape(4, 2, 2, 2, 2, 2, 10, 512)
    rows = [
        spread[:, :, :, :, r].transpose(3, 4, 0, 2, 1, 5, 6).reshape(2, 2, cols, 512)
        for r in range(2)
    ]
    kernel2 = conv2_weight.transpose(0, 1, 2, 4, 3).reshape(27 * 32, 512)
    held = run(cache_conv, ((128, cols), F32), (*rows, kernel2), 16)
    stats2 = run(functools.partial(row_stats, peers=peers), ((peers, 1, 128), F32), (gathered,))

    def at(y, l, h):
        return (y * n_l + l) * 2 + h

    down_h = []
    for y in range(n_y):
        for l in range(n_l):
            for h in range(2):
                if l < n_l - 1:
                    down_h.append((at(y, l, h), at(y, l + 1, h)))
                elif y < n_y - 1:
                    down_h.append((at(y, l, h), at(y + 1, 0, 1 - h)))
    up_h = [pair[::-1] for pair in down_h]
    old_above = lax.ppermute(rows[1], ("y", "l", "h"), down_h)
    old_below = lax.ppermute(rows[0], ("y", "l", "h"), up_h)
    row_above = lax.ppermute(gathered, ("y", "l", "h"), down_h)
    row_below = lax.ppermute(gathered, ("y", "l", "h"), up_h)
    stats2 = lax.all_to_all(stats2, space, 0, 0, tiled=True)
    affine2, bias_here = run(
        up_columns,
        [((512, 2), F32), ((128, 1), F32)],
        (norm2_gain[None], norm2_bias[None], conv2_bias[None]),
    )
    lhs = run(up_weights, ((3 * 32, 3 * 512), BF16), (kernel2,))
    out = run(
        functools.partial(up_conv, sizes=sizes),
        ((16, cols // 16, 128), BF16),
        (
            stats2,
            gathered,
            row_above,
            row_below,
            affine2,
            lhs,
            held,
            bias_here,
            old_above,
            old_below,
            kernel2,
        ),
        16,
    )
    out = lax.all_to_all(out, ("x", "h", "k"), 0, 0, tiled=True)
    out = out.reshape(16, 10, 2, 2, 32).transpose(2, 1, 3, 0, 4)
    return out.reshape(1, 2, 20, 512)


def solution(mesh):
    peers = mesh.shape["space"]
    n_l = 8 if peers % 8 == 0 else 2
    n_y = peers // n_l
    fine = Mesh(mesh.devices.reshape(n_y, n_l, 4, 2, 2), ("y", "l", "x", "h", "k"))
    space, chan = ("y", "l"), ("x", "h", "k")
    placed = (
        P(None, space, None, chan),
        P(None, space, None, chan),
        P(chan),
        P(chan),
        P(None, None, None, chan, None),
        P(chan),
        P(None, space, chan, None),
        P(),
        P(),
        P(None, None, None, None, chan),
        P(),
    )

    def body(*args):
        return on_device((n_y, n_l), *args)

    return jax.shard_map(
        body,
        mesh=fine,
        in_specs=placed,
        out_specs=P(None, space, chan, None),
        check_vma=False,
    )
```

```python
import functools

import jax
import jax.numpy as jnp
from jax import lax
from jax.experimental import pallas as pl
from jax.experimental.pallas import tpu as pltpu
from jax.sharding import Mesh
from jax.sharding import PartitionSpec as P


GS = 16
EPS = 1e-06
F32 = jnp.float32
BF16 = jnp.bfloat16
USE_KERNELS = True
FIRST_GRANT = 56


def run(fn, out_shapes, args, grant=8):
    if not USE_KERNELS:
        return fn(*args)
    n_a, single = len(args), isinstance(out_shapes, tuple)
    shapes = [out_shapes] if single else list(out_shapes)

    def body(*refs):
        outs = fn(*[r[...] for r in refs[:n_a]])
        outs = [outs] if single else outs
        for ref, value in zip(refs[n_a:], outs):
            ref[...] = value

    vmem = pl.BlockSpec(memory_space=pltpu.VMEM)
    res = pl.pallas_call(
        body,
        out_shape=[jax.ShapeDtypeStruct(s, d) for s, d in shapes],
        in_specs=[vmem] * n_a,
        out_specs=[vmem] * len(shapes),
        compiler_params=pltpu.CompilerParams(vmem_limit_bytes=grant << 20),
    )(*args)
    return res[0] if single else res


def preload(array):
    if not USE_KERNELS:
        return array
    return pl.pallas_call(
        lambda source, target: pltpu.sync_copy(source, target),
        out_shape=jax.ShapeDtypeStruct(array.shape, array.dtype),
        in_specs=[pl.BlockSpec(memory_space=pltpu.HBM)],
        out_specs=pl.BlockSpec(memory_space=pltpu.VMEM),
        compiler_params=pltpu.CompilerParams(vmem_limit_bytes=4 << 20),
    )(array)


def to_row(col):
    n = col.shape[0]
    eye = lax.broadcasted_iota(jnp.int32, (n, n), 0) == lax.broadcasted_iota(jnp.int32, (n, n), 1)
    return jnp.sum(jnp.where(eye, col, 0.0), axis=0, keepdims=True)


def to_col(row, repeat):
    n = row.shape[1]
    rows = lax.broadcasted_iota(jnp.int32, (n * repeat, n), 0)
    lanes = lax.broadcasted_iota(jnp.int32, (n * repeat, n), 1)
    pick = (rows >= lanes * repeat) & (rows < lanes * repeat + repeat)
    return jnp.sum(jnp.where(pick, row, 0.0), axis=1, keepdims=True)


def partial_stats(values, peers):
    rows, cols = values.shape
    groups = rows // GS
    x = values.astype(F32)
    mean = jnp.sum(jnp.sum(x, axis=1, keepdims=True).reshape(groups, GS, 1), axis=1) / (GS * cols)
    dev = x.reshape(groups, GS, cols) - mean[:, :, None]
    sq = jnp.sum(jnp.sum(dev * dev, axis=2, keepdims=True), axis=1)
    row = jnp.concatenate(
        [to_row(mean), to_row(sq), jnp.zeros((1, 128 - 2 * groups), F32)], axis=1
    )
    return jnp.broadcast_to(row[None], (peers, 1, 128))


def merge_stats(parts, groups, count):
    peers = parts.shape[0]
    means = parts[:, 0, :groups]
    sq = parts[:, 0, groups : 2 * groups]
    mean = jnp.sum(means, axis=0, keepdims=True) / peers
    gap = means - mean
    var = (jnp.sum(sq, axis=0, keepdims=True) + count * jnp.sum(gap * gap, axis=0, keepdims=True)) / (
        count * peers
    )
    return mean, lax.rsqrt(var + EPS)


def norm_silu(x, mean, scale, gain, bias):
    v = (x.astype(F32) - mean) * scale * gain + bias
    low = v < -80.0
    e = jnp.exp(jnp.where(low, v, -v))
    return jnp.where(low, v * e, v / (1.0 + jnp.where(low, 0.0, e)))


def wide_col(row):
    n = row.shape[1]
    return jnp.concatenate([to_col(row[:, i : i + 128], 1) for i in range(0, n, 128)], axis=0)


def pack(a):
    tail = jnp.concatenate([a[16 * i : 16 * i + 16, 128:] for i in range(4)], axis=1)
    return jnp.concatenate([a[:, :128], tail], axis=0)


def unpack(a):
    tail = jnp.concatenate([a[64:, 32 * i : 32 * i + 32] for i in range(4)], axis=0)
    return jnp.concatenate([a[:64], tail], axis=1)


def right(a):
    return jnp.concatenate([jnp.zeros((a.shape[0], 1), a.dtype), a[:, :-1]], axis=1)


def left(a):
    return jnp.concatenate([a[:, 1:], jnp.zeros((a.shape[0], 1), a.dtype)], axis=1)


def edges(sizes):
    n_y, n_l = sizes
    row = lax.axis_index("y") * n_l + lax.axis_index("l")
    return row > 0, row < n_y * n_l - 1


def first_pass(own, cache, gain, bias, late_bias, peers):
    cols = jnp.concatenate([to_col(v, 1) for v in (gain, bias, late_bias)], axis=1)
    return partial_stats(own, peers), jnp.concatenate([cache, own[None]], axis=0), cols


def mid_conv(parts, raw, above, below, affine, kernel, sizes):
    chans, cols = raw.shape[1:]
    groups = chans // GS
    mean, scale = merge_stats(parts, groups, GS * cols)
    mean, scale = to_col(mean, GS), to_col(scale, GS)
    gain, bias = affine[:, :1], affine[:, 1:2]
    has = edges(sizes)
    pieces = []
    for t in range(3):
        for dy, src in enumerate((above, raw, below)):
            x = src[t].astype(F32)
            if t == 2:
                x = norm_silu(x, mean, scale, gain, bias)
                if dy != 1:
                    x = jnp.where(has[0 if dy == 0 else 1], x, 0.0)
            pieces += [right(x).astype(BF16), x.astype(BF16), left(x).astype(BF16)]
    columns = jnp.concatenate(pieces, axis=0)
    out = jnp.dot(columns.T, kernel, preferred_element_type=F32).T
    blocks = []
    for x in range(4):
        for k in range(2):
            both = [out[(x * 4 + h * 2 + k) * 32 :][:32] for h in range(2)]
            blocks.append(pack(jnp.concatenate(both, axis=0)))
    return jnp.stack(blocks)


def fold(parts, own, affine):
    total = unpack(jnp.sum(parts, axis=0))
    extra = own.astype(F32) + affine[:, 2:3]
    zero = jnp.zeros_like(extra)
    first = lax.axis_index("h") == 0
    return pack(
        total
        + jnp.concatenate([jnp.where(first, extra, zero), jnp.where(first, zero, extra)], axis=0)
    )


def merge(mine, other):
    merged = (mine + other).astype(BF16)
    return jnp.broadcast_to(merged[None], (8,) + merged.shape)


def rows_of(gathered):
    blocks = [unpack(gathered[i].astype(F32)) for i in range(8)]
    return jnp.concatenate(
        [
            blocks[x * 2 + k][h * 32 : (h + 1) * 32]
            for x in range(4)
            for h in range(2)
            for k in range(2)
        ],
        axis=0,
    )


def row_stats(gathered, peers):
    return partial_stats(rows_of(gathered), peers)


def product(w, image):
    return lax.dot_general(w, image, (((1,), (1,)), ((), ())), preferred_element_type=F32)


def phases(even, odd):
    first = even[32:64] + odd[64:] + right(odd[:32])
    second = even[:32] + odd[32:64] + left(even[64:])
    return jnp.concatenate([first, second], axis=0)


def cache_conv(first, second, kernel):
    outs = []
    for o in range(2):
        sums = []
        for p in range(2):
            total = None
            for t in range(2):
                for r in range(2):
                    row = (t * 3 + r - o + 1) * 96
                    value = product(kernel[row : row + 96], (first, second)[r][t, p])
                    total = value if total is None else total + value
            sums.append(total)
        outs.append(phases(*sums))
    return jnp.concatenate(outs, axis=0)


def edge_conv(above, below, kernel):
    outs = []
    for image, dy in ((above, 0), (below, 2)):
        sums = [
            product(kernel[dy * 96 : dy * 96 + 96], image[0, p])
            + product(kernel[(3 + dy) * 96 : (4 + dy) * 96], image[1, p])
            for p in range(2)
        ]
        outs.append(phases(*sums))
    return jnp.concatenate(outs, axis=0)


def up_columns(gain, bias, out_bias):
    chan = lax.axis_index("x") * 4 + lax.axis_index("h") * 2 + lax.axis_index("k")
    rows = lax.broadcasted_iota(jnp.int32, (32, out_bias.shape[1]), 0)
    lanes = lax.broadcasted_iota(jnp.int32, (32, out_bias.shape[1]), 1)
    picked = jnp.sum(jnp.where(lanes == rows + chan * 32, out_bias, 0.0), axis=1, keepdims=True)
    return jnp.concatenate([wide_col(gain), wide_col(bias)], axis=1), jnp.concatenate(
        [picked] * 4, axis=0
    )


def up_weights(kernel):
    return jnp.concatenate(
        [kernel[(18 + dy * 3) * 32 : (21 + dy * 3) * 32] for dy in range(3)], axis=1
    )


def up_conv(parts, row, above, below, affine, lhs, held, edge, out_bias, sizes):
    row, above, below = rows_of(row), rows_of(above), rows_of(below)
    chans, cols = row.shape
    groups = chans // GS
    mean, scale = merge_stats(parts, groups, GS * cols)
    mean, scale = to_col(mean, GS), to_col(scale, GS)
    gain, bias = affine[:, :1], affine[:, 1:2]
    has = edges(sizes)

    def image(x, keep=None):
        v = norm_silu(x, mean, scale, gain, bias)
        if keep is not None:
            v = jnp.where(keep, v, 0.0)
        return v.astype(BF16)

    here = image(row)
    outs = []
    for images in ((image(above, has[0]), here, here), (here, here, image(below, has[1]))):
        prod = jnp.dot(lhs, jnp.concatenate(images, axis=0), preferred_element_type=F32)
        cut = [prod[dx * 32 : (dx + 1) * 32] for dx in range(3)]
        outs += [right(cut[0]) + cut[1] + cut[2], cut[0] + cut[1] + left(cut[2])]
    total = jnp.concatenate(outs, axis=0) + held
    total = total + edge
    total = (total + out_bias).T
    part = cols // 16
    return jnp.stack([total[c * part : (c + 1) * part] for c in range(16)]).astype(BF16)


def on_device(
    sizes,
    latent,
    cache_mid,
    norm1_gain,
    norm1_bias,
    conv1_weight,
    conv1_bias,
    cache_up,
    norm2_gain,
    norm2_bias,
    conv2_weight,
    conv2_bias,
):
    n_y, n_l = sizes
    peers = n_y * n_l
    cols, chans = latent.shape[2], latent.shape[3]
    sizes = (n_y, n_l)
    hi = lax.axis_index("h")
    space = ("y", "l")
    own = latent[0, 0].T
    stats, raw, affine = run(
        functools.partial(first_pass, peers=peers),
        [((peers, 1, 128), F32), ((3, chans, cols), BF16), ((chans, 3), F32)],
        (own, cache_mid[:, 0].transpose(0, 2, 1), norm1_gain[None], norm1_bias[None], conv1_bias[None]),
        FIRST_GRANT,
    )
    stats = lax.all_to_all(stats, space, 0, 0, tiled=True)
    down = [(i, i + 1) for i in range(peers - 1)]
    up = [(i + 1, i) for i in range(peers - 1)]
    above = lax.ppermute(raw, space, down)
    below = lax.ppermute(raw, space, up)
    partial = run(
        functools.partial(mid_conv, sizes=sizes),
        ((8, 80, 128), F32),
        (stats, raw, above, below, affine, preload(conv1_weight.reshape(27 * chans, 512))),
    )
    partial = lax.all_to_all(partial, ("x", "k"), 0, 0, tiled=True)
    mine = run(fold, ((80, 128), F32), (partial, own, affine))
    other = lax.ppermute(mine, "h", [(0, 1), (1, 0)])
    gathered = run(merge, ((8, 80, 128), BF16), (mine, other))
    gathered = lax.all_to_all(gathered, ("x", "k"), 0, 0, tiled=True)
    tile = cache_up.reshape(2, 2, 10, 2, 512).transpose(0, 1, 3, 2, 4)
    swapped = lax.ppermute(tile, "h", [(0, 1), (1, 0)])
    pair = jnp.where(hi == 0, jnp.stack([tile, swapped]), jnp.stack([swapped, tile]))
    copies = jnp.broadcast_to(pair[None], (8,) + pair.shape)
    spread = lax.all_to_all(copies, ("x", "k"), 0, 0, tiled=True)
    spread = spread.reshape(4, 2, 2, 2, 2, 2, 10, 512)
    rows = [
        spread[:, :, :, :, r].transpose(3, 4, 0, 2, 1, 5, 6).reshape(2, 2, cols, 512)
        for r in range(2)
    ]
    kernel2 = conv2_weight.transpose(0, 1, 2, 4, 3).reshape(27 * 32, 512)
    held = run(cache_conv, ((128, cols), F32), (*rows, kernel2))
    stats2 = run(functools.partial(row_stats, peers=peers), ((peers, 1, 128), F32), (gathered,))

    def at(y, l, h):
        return (y * n_l + l) * 2 + h

    down_h = []
    for y in range(n_y):
        for l in range(n_l):
            for h in range(2):
                if l < n_l - 1:
                    down_h.append((at(y, l, h), at(y, l + 1, h)))
                elif y < n_y - 1:
                    down_h.append((at(y, l, h), at(y + 1, 0, 1 - h)))
    up_h = [pair[::-1] for pair in down_h]
    old_above = lax.ppermute(rows[1], ("y", "l", "h"), down_h)
    old_below = lax.ppermute(rows[0], ("y", "l", "h"), up_h)
    row_above = lax.ppermute(gathered, ("y", "l", "h"), down_h)
    row_below = lax.ppermute(gathered, ("y", "l", "h"), up_h)
    stats2 = lax.all_to_all(stats2, space, 0, 0, tiled=True)
    edge = run(edge_conv, ((128, cols), F32), (old_above, old_below, kernel2))
    affine2, bias_here = run(
        up_columns,
        [((512, 2), F32), ((128, 1), F32)],
        (norm2_gain[None], norm2_bias[None], conv2_bias[None]),
    )
    lhs = run(up_weights, ((3 * 32, 3 * 512), BF16), (kernel2,))
    out = run(
        functools.partial(up_conv, sizes=sizes),
        ((16, cols // 16, 128), BF16),
        (
            stats2,
            gathered,
            row_above,
            row_below,
            affine2,
            lhs,
            held,
            edge,
            bias_here,
        ),
    )
    out = lax.all_to_all(out, ("x", "h", "k"), 0, 0, tiled=True)
    out = out.reshape(16, 10, 2, 2, 32).transpose(2, 1, 3, 0, 4)
    return out.reshape(1, 2, 20, 512)


def solution(mesh):
    peers = mesh.shape["space"]
    n_l = 8 if peers % 8 == 0 else 2
    n_y = peers // n_l
    fine = Mesh(mesh.devices.reshape(n_y, n_l, 4, 2, 2), ("y", "l", "x", "h", "k"))
    space, chan = ("y", "l"), ("x", "h", "k")
    placed = (
        P(None, space, None, chan),
        P(None, space, None, chan),
        P(chan),
        P(chan),
        P(None, None, None, chan, None),
        P(chan),
        P(None, space, chan, None),
        P(),
        P(),
        P(None, None, None, None, chan),
        P(),
    )

    def body(*args):
        return on_device((n_y, n_l), *args)

    return jax.shard_map(
        body,
        mesh=fine,
        in_specs=placed,
        out_specs=P(None, space, chan, None),
        check_vma=False,
    )
```

```python
import functools

import jax
import jax.numpy as jnp
from jax import lax
from jax.experimental import pallas as pl
from jax.experimental.pallas import tpu as pltpu
from jax.sharding import Mesh
from jax.sharding import PartitionSpec as P


GS = 16
EPS = 1e-06
F32 = jnp.float32
BF16 = jnp.bfloat16
USE_KERNELS = True
FIRST_GRANT = 56


def run(fn, out_shapes, args, grant=8):
    if not USE_KERNELS:
        return fn(*args)
    n_a, single = len(args), isinstance(out_shapes, tuple)
    shapes = [out_shapes] if single else list(out_shapes)

    def body(*refs):
        outs = fn(*[r[...] for r in refs[:n_a]])
        outs = [outs] if single else outs
        for ref, value in zip(refs[n_a:], outs):
            ref[...] = value

    vmem = pl.BlockSpec(memory_space=pltpu.VMEM)
    res = pl.pallas_call(
        body,
        out_shape=[jax.ShapeDtypeStruct(s, d) for s, d in shapes],
        in_specs=[vmem] * n_a,
        out_specs=[vmem] * len(shapes),
        compiler_params=pltpu.CompilerParams(vmem_limit_bytes=grant << 20),
    )(*args)
    return res[0] if single else res


def preload(array):
    if not USE_KERNELS:
        return array
    return pl.pallas_call(
        lambda source, target: pltpu.sync_copy(source, target),
        out_shape=jax.ShapeDtypeStruct(array.shape, array.dtype),
        in_specs=[pl.BlockSpec(memory_space=pltpu.HBM)],
        out_specs=pl.BlockSpec(memory_space=pltpu.VMEM),
        compiler_params=pltpu.CompilerParams(vmem_limit_bytes=4 << 20),
    )(array)


def to_row(col):
    n = col.shape[0]
    eye = lax.broadcasted_iota(jnp.int32, (n, n), 0) == lax.broadcasted_iota(jnp.int32, (n, n), 1)
    return jnp.sum(jnp.where(eye, col, 0.0), axis=0, keepdims=True)


def to_col(row, repeat):
    n = row.shape[1]
    rows = lax.broadcasted_iota(jnp.int32, (n * repeat, n), 0)
    lanes = lax.broadcasted_iota(jnp.int32, (n * repeat, n), 1)
    pick = (rows >= lanes * repeat) & (rows < lanes * repeat + repeat)
    return jnp.sum(jnp.where(pick, row, 0.0), axis=1, keepdims=True)


def partial_stats(values, peers):
    rows, cols = values.shape
    groups = rows // GS
    x = values.astype(F32)
    mean = jnp.sum(jnp.sum(x, axis=1, keepdims=True).reshape(groups, GS, 1), axis=1) / (GS * cols)
    dev = x.reshape(groups, GS, cols) - mean[:, :, None]
    sq = jnp.sum(jnp.sum(dev * dev, axis=2, keepdims=True), axis=1)
    row = jnp.concatenate(
        [to_row(mean), to_row(sq), jnp.zeros((1, 128 - 2 * groups), F32)], axis=1
    )
    return jnp.broadcast_to(row[None], (peers, 1, 128))


def merge_stats(parts, groups, count):
    peers = parts.shape[0]
    means = parts[:, 0, :groups]
    sq = parts[:, 0, groups : 2 * groups]
    mean = jnp.sum(means, axis=0, keepdims=True) / peers
    gap = means - mean
    var = (jnp.sum(sq, axis=0, keepdims=True) + count * jnp.sum(gap * gap, axis=0, keepdims=True)) / (
        count * peers
    )
    return mean, lax.rsqrt(var + EPS)


def norm_silu(x, mean, scale, gain, bias):
    v = (x.astype(F32) - mean) * scale * gain + bias
    low = v < -80.0
    e = jnp.exp(jnp.where(low, v, -v))
    return jnp.where(low, v * e, v / (1.0 + jnp.where(low, 0.0, e)))


def wide_col(row):
    n = row.shape[1]
    return jnp.concatenate([to_col(row[:, i : i + 128], 1) for i in range(0, n, 128)], axis=0)


def pack(a):
    tail = jnp.concatenate([a[16 * i : 16 * i + 16, 128:] for i in range(4)], axis=1)
    return jnp.concatenate([a[:, :128], tail], axis=0)


def unpack(a):
    tail = jnp.concatenate([a[64:, 32 * i : 32 * i + 32] for i in range(4)], axis=0)
    return jnp.concatenate([a[:64], tail], axis=1)


def right(a):
    return jnp.concatenate([jnp.zeros((a.shape[0], 1), a.dtype), a[:, :-1]], axis=1)


def left(a):
    return jnp.concatenate([a[:, 1:], jnp.zeros((a.shape[0], 1), a.dtype)], axis=1)


def edges(sizes):
    n_y, n_l = sizes
    row = lax.axis_index("y") * n_l + lax.axis_index("l")
    return row > 0, row < n_y * n_l - 1


def first_pass(own, cache, gain, bias, late_bias, peers):
    cols = jnp.concatenate([to_col(v, 1) for v in (gain, bias, late_bias)], axis=1)
    return partial_stats(own, peers), jnp.concatenate([cache, own[None]], axis=0), cols


def mid_conv(parts, raw, above, below, affine, kernel, sizes):
    chans, cols = raw.shape[1:]
    groups = chans // GS
    mean, scale = merge_stats(parts, groups, GS * cols)
    mean, scale = to_col(mean, GS), to_col(scale, GS)
    gain, bias = affine[:, :1], affine[:, 1:2]
    has = edges(sizes)
    pieces = []
    for t in range(3):
        for dy, src in enumerate((above, raw, below)):
            x = src[t].astype(F32)
            if t == 2:
                x = norm_silu(x, mean, scale, gain, bias)
                if dy != 1:
                    x = jnp.where(has[0 if dy == 0 else 1], x, 0.0)
            pieces += [right(x).astype(BF16), x.astype(BF16), left(x).astype(BF16)]
    columns = jnp.concatenate(pieces, axis=0)
    out = jnp.dot(columns.T, kernel, preferred_element_type=F32).T
    blocks = []
    for x in range(4):
        for k in range(2):
            both = [out[(x * 4 + h * 2 + k) * 32 :][:32] for h in range(2)]
            blocks.append(pack(jnp.concatenate(both, axis=0)))
    return jnp.stack(blocks)


def fold(parts, own, affine):
    total = unpack(jnp.sum(parts, axis=0))
    extra = own.astype(F32) + affine[:, 2:3]
    zero = jnp.zeros_like(extra)
    first = lax.axis_index("h") == 0
    return pack(
        total
        + jnp.concatenate([jnp.where(first, extra, zero), jnp.where(first, zero, extra)], axis=0)
    )


def merge(mine, other):
    merged = (mine + other).astype(BF16)
    return jnp.broadcast_to(merged[None], (8,) + merged.shape)


def rows_of(gathered):
    blocks = [unpack(gathered[i].astype(F32)) for i in range(8)]
    return jnp.concatenate(
        [
            blocks[x * 2 + k][h * 32 : (h + 1) * 32]
            for x in range(4)
            for h in range(2)
            for k in range(2)
        ],
        axis=0,
    )


def row_stats(gathered, peers):
    return partial_stats(rows_of(gathered), peers)


def join_rows(gathered, to_above, to_below):
    return (
        jnp.concatenate([gathered, to_above], axis=0),
        jnp.concatenate([gathered, to_below], axis=0),
    )


def halves(a):
    a = pack(a)
    high = a.astype(BF16)
    return jnp.stack([high, (a - high.astype(F32)).astype(BF16)])


def whole(blocks):
    return unpack(blocks[0].astype(F32) + blocks[1].astype(F32))


def taps(prod):
    return [[prod[(dy * 3 + dx) * 32 : (dy * 3 + dx + 1) * 32] for dx in range(3)] for dy in range(3)]


def cache_conv(images, kernel):
    per = 9 * 32
    sums = {}

    def add(key, value):
        sums[key] = sums[key] + value if key in sums else value

    for t in range(2):
        w = kernel[t * per : (t + 1) * per]
        for r in range(2):
            even, odd = (
                taps(
                    lax.dot_general(
                        w, images[t, r, p], (((1,), (1,)), ((), ())), preferred_element_type=F32
                    )
                )
                for p in range(2)
            )
            for dy in range(3):
                o = r + 1 - dy
                add((o, "m", 0), even[dy][1] + odd[dy][2])
                add((o, "r", 0), odd[dy][0])
                add((o, "m", 1), even[dy][0] + odd[dy][1])
                add((o, "l", 1), even[dy][2])

    def out(o):
        return jnp.concatenate(
            [
                sums[(o, "m", 0)] + right(sums[(o, "r", 0)]),
                sums[(o, "m", 1)] + left(sums[(o, "l", 1)]),
            ],
            axis=0,
        )

    return jnp.concatenate([out(0), out(1)], axis=0), halves(out(-1)), halves(out(2))


def up_columns(gain, bias, out_bias):
    chan = lax.axis_index("x") * 4 + lax.axis_index("h") * 2 + lax.axis_index("k")
    rows = lax.broadcasted_iota(jnp.int32, (32, out_bias.shape[1]), 0)
    lanes = lax.broadcasted_iota(jnp.int32, (32, out_bias.shape[1]), 1)
    picked = jnp.sum(jnp.where(lanes == rows + chan * 32, out_bias, 0.0), axis=1, keepdims=True)
    return jnp.concatenate([wide_col(gain), wide_col(bias)], axis=1), jnp.concatenate(
        [picked] * 4, axis=0
    )


def up_weights(kernel):
    return jnp.concatenate(
        [kernel[(18 + dy * 3) * 32 : (21 + dy * 3) * 32] for dy in range(3)], axis=1
    )


def up_conv(parts, row, above, below, affine, lhs, held, out_bias, sizes):
    from_above, from_below = whole(above[8:]), whole(below[8:])
    row, above, below = rows_of(row), rows_of(above[:8]), rows_of(below[:8])
    chans, cols = row.shape
    groups = chans // GS
    mean, scale = merge_stats(parts, groups, GS * cols)
    mean, scale = to_col(mean, GS), to_col(scale, GS)
    gain, bias = affine[:, :1], affine[:, 1:2]
    has = edges(sizes)

    def image(x, keep=None):
        v = norm_silu(x, mean, scale, gain, bias)
        if keep is not None:
            v = jnp.where(keep, v, 0.0)
        return v.astype(BF16)

    here = image(row)
    outs = []
    for images in ((image(above, has[0]), here, here), (here, here, image(below, has[1]))):
        prod = jnp.dot(lhs, jnp.concatenate(images, axis=0), preferred_element_type=F32)
        cut = [prod[dx * 32 : (dx + 1) * 32] for dx in range(3)]
        outs += [right(cut[0]) + cut[1] + cut[2], cut[0] + cut[1] + left(cut[2])]
    total = jnp.concatenate(outs, axis=0) + held
    total = total + jnp.concatenate([from_above, from_below], axis=0)
    total = (total + out_bias).T
    part = cols // 16
    return jnp.stack([total[c * part : (c + 1) * part] for c in range(16)]).astype(BF16)


def on_device(
    sizes,
    latent,
    cache_mid,
    norm1_gain,
    norm1_bias,
    conv1_weight,
    conv1_bias,
    cache_up,
    norm2_gain,
    norm2_bias,
    conv2_weight,
    conv2_bias,
):
    n_y, n_l = sizes
    peers = n_y * n_l
    cols, chans = latent.shape[2], latent.shape[3]
    sizes = (n_y, n_l)
    hi = lax.axis_index("h")
    space = ("y", "l")
    own = latent[0, 0].T
    stats, raw, affine = run(
        functools.partial(first_pass, peers=peers),
        [((peers, 1, 128), F32), ((3, chans, cols), BF16), ((chans, 3), F32)],
        (own, cache_mid[:, 0].transpose(0, 2, 1), norm1_gain[None], norm1_bias[None], conv1_bias[None]),
        FIRST_GRANT,
    )
    stats = lax.all_to_all(stats, space, 0, 0, tiled=True)
    down = [(i, i + 1) for i in range(peers - 1)]
    up = [(i + 1, i) for i in range(peers - 1)]
    above = lax.ppermute(raw, space, down)
    below = lax.ppermute(raw, space, up)
    partial = run(
        functools.partial(mid_conv, sizes=sizes),
        ((8, 80, 128), F32),
        (stats, raw, above, below, affine, preload(conv1_weight.reshape(27 * chans, 512))),
    )
    partial = lax.all_to_all(partial, ("x", "k"), 0, 0, tiled=True)
    mine = run(fold, ((80, 128), F32), (partial, own, affine))
    other = lax.ppermute(mine, "h", [(0, 1), (1, 0)])
    gathered = run(merge, ((8, 80, 128), BF16), (mine, other))
    gathered = lax.all_to_all(gathered, ("x", "k"), 0, 0, tiled=True)
    tile = cache_up.reshape(2, 2, 10, 2, 512).transpose(0, 1, 3, 2, 4)
    swapped = lax.ppermute(tile, "h", [(0, 1), (1, 0)])
    pair = jnp.where(hi == 0, jnp.stack([tile, swapped]), jnp.stack([swapped, tile]))
    copies = jnp.broadcast_to(pair[None], (8,) + pair.shape)
    spread = lax.all_to_all(copies, ("x", "k"), 0, 0, tiled=True)
    images = (
        spread.reshape(4, 2, 2, 2, 2, 2, 10, 512)
        .transpose(3, 4, 5, 0, 2, 1, 6, 7)
        .reshape(2, 2, 2, cols, 512)
    )
    kernel2 = conv2_weight.transpose(0, 1, 2, 4, 3).reshape(27 * 32, 512)
    held, to_above, to_below = run(
        cache_conv,
        [((128, cols), F32), ((2, 80, 128), BF16), ((2, 80, 128), BF16)],
        (images, kernel2),
        16,
    )
    stats2 = run(functools.partial(row_stats, peers=peers), ((peers, 1, 128), F32), (gathered,))
    going_up, going_down = run(
        join_rows, [((10, 80, 128), BF16), ((10, 80, 128), BF16)], (gathered, to_above, to_below)
    )
    row_above = lax.ppermute(going_down, space, down)
    row_below = lax.ppermute(going_up, space, up)
    stats2 = lax.all_to_all(stats2, space, 0, 0, tiled=True)
    affine2, bias_here = run(
        up_columns,
        [((512, 2), F32), ((128, 1), F32)],
        (norm2_gain[None], norm2_bias[None], conv2_bias[None]),
    )
    lhs = run(up_weights, ((3 * 32, 3 * 512), BF16), (kernel2,))
    out = run(
        functools.partial(up_conv, sizes=sizes),
        ((16, cols // 16, 128), BF16),
        (
            stats2,
            gathered,
            row_above,
            row_below,
            affine2,
            lhs,
            held,
            bias_here,
        ),
        16,
    )
    out = lax.all_to_all(out, ("x", "h", "k"), 0, 0, tiled=True)
    out = out.reshape(16, 10, 2, 2, 32).transpose(2, 1, 3, 0, 4)
    return out.reshape(1, 2, 20, 512)


def solution(mesh):
    peers = mesh.shape["space"]
    n_l = 8 if peers % 8 == 0 else 2
    n_y = peers // n_l
    fine = Mesh(mesh.devices.reshape(n_y, n_l, 4, 2, 2), ("y", "l", "x", "h", "k"))
    space, chan = ("y", "l"), ("x", "h", "k")
    placed = (
        P(None, space, None, chan),
        P(None, space, None, chan),
        P(chan),
        P(chan),
        P(None, None, None, chan, None),
        P(chan),
        P(None, space, chan, None),
        P(),
        P(),
        P(None, None, None, None, chan),
        P(),
    )

    def body(*args):
        return on_device((n_y, n_l), *args)

    return jax.shard_map(
        body,
        mesh=fine,
        in_specs=placed,
        out_specs=P(None, space, chan, None),
        check_vma=False,
    )
```
